128 devices in a mesh: dp: 8 (over x, y_hi), seq: 16 (over y_lo, z, core).
Axes of the slice: x: 4, y: 4 (y_hi: 2, y_lo: 2; y = y_hi * 2 + y_lo), z: 4, core: 2. Of those that a mesh axis runs over, the one named last changes fastest.
Arguments:
- caption_states: bfloat16 [8, 128, 4096], P('dp', None, 'seq'), may hold values from -1600 to 1600
- caption_gain: float32 [4096], P('seq'), may hold values from 0.25 to 2.5
- text_proj: bfloat16 [4096, 4608], P('seq'), may hold values from -0.09375 to 0.09375
- caption_len: int32 [8], P('dp'), may hold values from 1 to 128, 640 in all
- slot_source: int32 [8, 128], P('dp'), may hold values from 0 to 127, each once within a row
- query_gain: float32 [128], replicated, may hold values from 0.5 to 2
- key_gain: float32 [128], replicated, may hold values from 0.5 to 2
- image_q: bfloat16 [8, 2048, 1536], P('dp', 'seq'), may hold values from -34 to 34
- image_k: bfloat16 [8, 2048, 1536], P('dp', 'seq'), may hold values from -6.5 to 6.5
- image_v: bfloat16 [8, 2048, 1536], P('dp', 'seq'), may hold values from -6 to 6
- out_weight: bfloat16 [3072, 1536], replicated, may hold values from -0.15625 to 0.15625
- gate: float32 [8, 3072], P('dp'), may hold values from -4 to 4
- d_out: bfloat16 [8, 2048, 3072], P('dp', 'seq'), may hold values from -2.5 to 2.5
Outputs:
- image_out: bfloat16 [8, 2048, 3072], P('dp', 'seq')
- text_attn: bfloat16 [8, 128, 1536], P('dp', 'seq')
- d_attn: bfloat16 [8, 2048, 1536], P('dp', 'seq')
- grad_wo: float32 [3072, 1536], P(('dp', 'seq'))
- grad_gate: float32 [8, 3072], P('dp', 'seq')
The draws below stay inside these ranges and needn't reach their ends.
Inputs may be any that keep to these rules, and one draw needn't show every extreme that they name: `caption_len`: caption lengths in tokens; the longest is 128. `slot_source`: each row is a permutation: every caption row of the sequence sits in exactly one slot; slots whose row is not below the caption's length are padding.
All inputs are finite; a program needn't handle non-finite values. No bound on the sum of `caption_len` on one device may be relied on, other than what follows from the above.
Results may differ from the reference program's by a relative error of at most 0.0095.
Values may be sent and summed in bfloat16 or wider, within the bound.
A program may use at most 128 MiB of HBM per device.

```python
import math
import jax
import jax.numpy as jnp
import numpy as np
from jax import lax

D = 3072
HD = 128
DT5 = 4096
TXT_DEV = 8
INNER = 1536
IMG_LEN = 2048
TXT_TOTAL = 128
BATCH = 8
N_DP = 8
N_SEQ = 16


def draw_caption_states(key, part):
    key_base = jax.random.fold_in(key, 1)
    key_cols = jax.random.fold_in(key, 2)
    key_rows = jax.random.fold_in(key, 3)
    shape = (BATCH, TXT_TOTAL, DT5)
    position = jnp.arange(DT5, dtype=jnp.float32) / (DT5 - 1)
    base = jnp.clip(jax.random.normal(key_base, shape, jnp.float32), -4.0, 4.0)
    rising = 3.0 ** position
    column_scale = rising * jnp.exp(math.log(10.0) * jax.random.uniform(key_cols, (DT5,), jnp.float32))
    row_scale = jnp.exp(math.log(10.0) * jax.random.uniform(key_rows, (BATCH, TXT_TOTAL, 1), jnp.float32))
    return (base * column_scale * row_scale).astype(jnp.bfloat16)


def paired_queries_keys(key):
    base_key = jax.random.fold_in(key, 11)
    query_key = jax.random.fold_in(base_key, 1)
    key_key = jax.random.fold_in(base_key, 2)
    shape = (BATCH, IMG_LEN, INNER)
    queries = 1.6 * jnp.clip(jax.random.normal(query_key, shape, jnp.float32), -4.0, 4.0)
    key_rows = 1.6 * jnp.clip(jax.random.normal(key_key, shape, jnp.float32), -4.0, 4.0)
    return (queries, key_rows)


def draw_image_q(key, part):
    queries, key_rows = paired_queries_keys(key)
    return queries.astype(jnp.bfloat16)


def draw_image_k(key, part):
    queries, key_rows = paired_queries_keys(key)
    return key_rows.astype(jnp.bfloat16)


def raised(entries, own_key, source, target, parts, factor):
    owner, partner = [(jnp.arange(entries.shape[axis_at]) // (entries.shape[axis_at] // parts)).reshape([-1 if axis == axis_at else 1 for axis in range(entries.ndim)]) for axis_at in (source, target)]
    chosen = jax.random.permutation(own_key, parts)[partner]
    strong = (owner == chosen) | (owner == (partner + parts // 2) % parts)
    return jnp.where(strong, factor * entries, entries)


def levels(key, extent, shards, least, high):
    def one(dim, parts):
        heights = jax.random.uniform(jax.random.fold_in(jax.random.fold_in(key, 6), dim), (parts,), jnp.float32, least / len(shards), high / len(shards))
        return jnp.repeat(jnp.exp(heights), extent[dim] // parts).reshape((-1,) + (1,) * (len(extent) - dim - 1))

    loudness = one(*shards[0])
    for cut in shards[1:]:
        loudness = loudness * one(*cut)
    return loudness


def length_profile(number_of, total, reach, lean):
    portions = [(1 << 20) // math.isqrt(grade ** lean) + 1 for grade in range(2, number_of + 1)]
    surplus, holding = total - reach - (number_of - 1), [1] * (number_of - 1)
    while surplus > 0:
        candidates = [i for i in range(number_of - 1) if holding[i] < reach]
        whole, remaining = sum([portions[i] for i in candidates]), surplus
        for i in candidates:
            more = min(reach - holding[i], max(1, remaining * portions[i] // whole), surplus)
            holding[i] = holding[i] + more
            surplus = surplus - more
    return np.array([reach] + holding)


def ragged_sizes(stream_key, count, total, limit, slope):
    if count == 2:
        one = jax.random.randint(stream_key, (), max(1, total - limit), min(limit, total - 1) + 1)
        return jnp.stack([one, total - one])
    lengths = jnp.asarray(length_profile(count, total, limit, slope), jnp.int32)
    couples = (count - 1) // 2
    donor, receiver = lengths[1:1 + 2 * couples:2], lengths[2:2 + 2 * couples:2]
    room = jnp.minimum(donor - 1, limit - receiver)
    shifted = jax.random.randint(jax.random.fold_in(stream_key, 1), (couples,), 0, 1 << 20) % (room + 1)
    lengths = lengths.at[1:1 + 2 * couples:2].set(donor - shifted).at[2:2 + 2 * couples:2].set(receiver + shifted)
    return lengths[jax.random.permutation(jax.random.fold_in(stream_key, 2), count)]


def scatter_about(own_key, shape, deviation, most, shards=(), kind=jnp.bfloat16):
    values = deviation * jax.random.normal(own_key, shape, jnp.float32)
    if shards:
        values = values * levels(own_key, shape, shards, -0.22, 0.18)
    return jnp.clip(values, -most, most).astype(kind)


def noise_with(rng, extent, spread, limit, pieces, heavy, held_as=jnp.bfloat16):
    result = spread * jax.random.normal(rng, extent, jnp.float32)
    if pieces:
        result = result * levels(rng, extent, pieces, -0.22, 0.18)
    return jnp.clip(raised(result, jax.random.fold_in(rng, 3), *heavy), -limit, limit).astype(held_as)


def setup_inputs(seed: int = 0) -> dict:
    seeds = jax.random.split(jax.random.key(seed), 14)
    caption_states = draw_caption_states(jax.random.fold_in(seeds[13], 71), 0)
    caption_gain = jnp.clip(jnp.exp(math.log(2.5) - 2.3025851 * jax.random.uniform(seeds[1], (DT5,), jnp.float32) ** levels(seeds[1], (DT5,), ((0, 16),), -0.2, 0.2)), 0.25, 2.5)
    text_proj = scatter_about(seeds[2], (DT5, 3 * INNER), DT5 ** -0.5, 0.09375, ((0, 16),))
    caption_len = ragged_sizes(seeds[3], BATCH, N_DP * TXT_DEV * N_SEQ * 5 // 8, TXT_DEV * N_SEQ, 1).astype(jnp.int32)
    slot_source = jax.vmap(lambda own: jax.random.permutation(own, TXT_TOTAL))(jax.random.split(seeds[4], BATCH)).reshape((BATCH, TXT_TOTAL)).astype(jnp.int32)
    query_gain = jnp.clip(jnp.exp(jax.random.uniform(seeds[5], (HD,), jnp.float32, math.log(0.5), math.log(2.0))), 0.5, 2.0)
    key_gain = jnp.clip(jnp.exp(jax.random.uniform(seeds[6], (HD,), jnp.float32, math.log(0.5), math.log(2.0))), 0.5, 2.0)
    image_q = draw_image_q(jax.random.fold_in(seeds[13], 71), 0)
    image_k = draw_image_k(jax.random.fold_in(seeds[13], 71), 0)
    image_v = scatter_about(seeds[9], (BATCH, IMG_LEN, INNER), 1.0, 6.0, ((0, 8), (1, 16)))
    out_weight = scatter_about(seeds[10], (D, INNER), INNER ** -0.5, 0.15625)
    gate = scatter_about(seeds[11], (BATCH, D), 1.0, 4.0, ((0, 8),), jnp.float32)
    d_out = noise_with(seeds[12], (BATCH, IMG_LEN, D), (16 * (N_DP * IMG_LEN) ** -0.5), 2.5, ((0, 8), (1, 16)), (1, 2, 16, 2.0))
    return {"caption_states": caption_states, "caption_gain": caption_gain, "text_proj": text_proj, "caption_len": caption_len, "slot_source": slot_source, "query_gain": query_gain, "key_gain": key_gain, "image_q": image_q, "image_k": image_k, "image_v": image_v, "out_weight": out_weight, "gate": gate, "d_out": d_out}


def head_norm(values_in, gain_vec):
    shaped = values_in.reshape(values_in.shape[:-1] + (-1, gain_vec.shape[0]))
    normed = shaped * lax.rsqrt(lax.optimization_barrier(jnp.mean(shaped * shaped, axis=-1, keepdims=True)) + 1e-06) * gain_vec
    return normed.reshape(values_in.shape)

def reference(caption_states, caption_gain, text_proj, caption_len, slot_source, query_gain, key_gain, image_q, image_k, image_v, out_weight, gate, d_out):
    batch_count, slot_total, enc_width = caption_states.shape
    inner_width = image_q.shape[2]
    head_size = query_gain.shape[0]
    image_rows = image_q.shape[1]
    model_width = out_weight.shape[0]
    states = caption_states.astype(jnp.float32)
    scaled = (states * caption_gain).astype(jnp.bfloat16)
    raw = jnp.dot(scaled.reshape(-1, enc_width), text_proj, preferred_element_type=jnp.float32).reshape(batch_count, slot_total, -1)
    rate = lax.rsqrt(lax.optimization_barrier(jnp.sum(states * states, axis=-1)) / enc_width + 1e-06)
    proj = raw * rate[..., None]
    proj = jnp.take_along_axis(proj, slot_source.astype(jnp.int32)[..., None], axis=1)
    valid = slot_source < caption_len[:, None]
    text_q = head_norm(proj[..., :inner_width], query_gain).astype(jnp.bfloat16)
    text_k = head_norm(proj[..., inner_width:2 * inner_width], key_gain).astype(jnp.bfloat16)
    text_v = proj[..., 2 * inner_width:].astype(jnp.bfloat16)
    queries = jnp.concatenate([image_q, text_q], axis=1)
    key_rows = jnp.concatenate([image_k, text_k], axis=1)
    value_rows = jnp.concatenate([image_v, text_v], axis=1)
    allowed = jnp.concatenate([jnp.ones((batch_count, image_rows), dtype=jnp.bool_), valid], axis=1)

    def attend_sequence(packed):
        query_seq, key_seq, value_seq, allowed_seq = packed
        joint = query_seq.shape[0]
        query_heads = jnp.transpose(query_seq.astype(jnp.float32).reshape(joint, -1, head_size), (1, 0, 2))
        key_heads = jnp.transpose(key_seq.astype(jnp.float32).reshape(joint, -1, head_size), (1, 0, 2))
        value_heads = jnp.transpose(value_seq.astype(jnp.float32).reshape(joint, -1, head_size), (1, 0, 2))

        def one_head(head_pack):
            query_one, key_one, value_one = head_pack
            scores = jnp.dot(query_one, key_one.T, preferred_element_type=jnp.float32) * head_size ** (-0.5)
            scores = jnp.where(allowed_seq[None, :], scores, -1e+30)
            row_max = lax.optimization_barrier(jnp.max(scores, axis=-1, keepdims=True))
            probs = jnp.where(allowed_seq[None, :], jnp.exp(scores - row_max), 0.0)
            denom = lax.optimization_barrier(jnp.sum(probs, axis=-1))
            probs_low = lax.optimization_barrier(probs.astype(jnp.bfloat16)).astype(jnp.float32)
            summed = jnp.dot(probs_low, value_one, preferred_element_type=jnp.float32)
            return summed / denom[:, None]
        output = lax.map(one_head, (query_heads, key_heads, value_heads))
        return jnp.transpose(output, (1, 0, 2)).reshape(joint, inner_width).astype(jnp.bfloat16)
    attn = lax.map(attend_sequence, (queries, key_rows, value_rows, allowed))
    image_attn = attn[:, :image_rows]
    text_attn = jnp.where(valid[..., None], attn[:, image_rows:], jnp.zeros((), jnp.bfloat16))
    projected = jnp.dot(image_attn.reshape(-1, inner_width), out_weight.T, preferred_element_type=jnp.float32).reshape(batch_count, image_rows, model_width)
    image_out = (gate[:, None, :] * projected).astype(jnp.bfloat16)
    cotangent = d_out.astype(jnp.float32)
    gated_grad = (gate[:, None, :] * cotangent).astype(jnp.bfloat16)
    d_attn = jnp.dot(gated_grad.reshape(-1, model_width), out_weight, preferred_element_type=jnp.float32).reshape(batch_count, image_rows, inner_width).astype(jnp.bfloat16)
    grad_wo = jnp.dot(gated_grad.reshape(-1, model_width).T, image_attn.reshape(-1, inner_width), preferred_element_type=jnp.float32)
    grad_gate = lax.optimization_barrier(jnp.sum(projected * cotangent, axis=1))
    return (image_out, text_attn, d_attn, grad_wo, grad_gate)
```

```python
import functools
import math

import jax
import jax.numpy as jnp
from jax import lax
from jax.experimental import pallas as pl
from jax.experimental.pallas import tpu as pltpu
from jax.sharding import PartitionSpec as P

EPS = 1e-06
NEG_BIG = -1e30
NY, NZ, NC = 2, 4, 2
NQ = NY * NC
F32 = jnp.float32
BF16 = jnp.bfloat16
NT = (((1,), (1,)), ((), ()))


def joint_kernel(
    n_dp,
    states_ref,
    gain_ref,
    text_proj_hbm,
    src_col_ref,
    src_row_ref,
    clen_ref,
    qgain_ref,
    kgain_ref,
    q_hbm,
    k_hbm,
    v_hbm,
    wo_hbm,
    gate_ref,
    dout_hbm,
    image_out_ref,
    text_attn_ref,
    d_attn_ref,
    grad_wo_ref,
    grad_gate_ref,
    tp,
    wo,
    dout,
    part,
    tbuf,
    qi,
    qt,
    kv,
    g,
    gtf,
    gt,
    gt_all,
    a_all,
    a_rows,
    tsend,
    trecv,
    psend,
    precv,
    fsend,
    fin,
    gsend,
    grecv,
    load_sem,
    loc_sem,
    kvq_s,
    kvq_r,
    fwd_s,
    fwd_r,
    txp_s,
    txp_r,
    txkv_s,
    txkv_r,
    g1_s,
    g1_r,
    gz_s,
    gz_r,
    aret_s,
    aret_r,
    tret_s,
    tret_r,
    apl_s,
    apl_r,
    dp_s,
    dp_r,
    fin_s,
    fin_r,
    gg_s,
    gg_r,
):
    dp = lax.axis_index("dp")
    me = lax.axis_index("seq")
    n_seq = NY * NZ * NC
    y = me // (NZ * NC)
    z = (me // NC) % NZ
    c = me % NC
    q = y * NC + c
    rows, inner = a_rows.shape[1], NZ * a_rows.shape[2]
    hg = a_rows.shape[2]
    head = 128
    n_heads = hg // head
    d_model = dout.shape[1]
    slots = src_row_ref.shape[1]
    tq = slots // NQ
    ts = tq // NZ
    image_keys = n_seq * rows
    blk = gt.shape[2]
    piece = blk // NZ

    def at_z(z_to):
        return y * (NZ * NC) + z_to * NC + c

    s_y = (1 - y) * (NZ * NC) + z * NC + c
    s_c = y * (NZ * NC) + z * NC + (1 - c)
    s_d = (1 - y) * (NZ * NC) + z * NC + (1 - c)
    q_y = (1 - y) * NC + c
    q_c = y * NC + (1 - c)
    q_d = (1 - y) * NC + (1 - c)

    def to_seq(src, dst, ss, rs, target):
        return pltpu.make_async_remote_copy(
            src_ref=src,
            dst_ref=dst,
            send_sem=ss,
            recv_sem=rs,
            device_id={"seq": target},
            device_id_type=pl.DeviceIdType.MESH,
        )

    load_tp = pltpu.make_async_copy(text_proj_hbm, tp, load_sem.at[0])
    load_dout = pltpu.make_async_copy(dout_hbm, dout, load_sem.at[1])
    load_wo = pltpu.make_async_copy(wo_hbm, wo, load_sem.at[2])
    load_tp.start()
    load_dout.start()
    load_wo.start()

    def col(index):
        return pl.ds(pl.multiple_of(index * hg, 128), hg)

    def kv_rows(q_from, z_from):
        return pl.ds(pl.multiple_of((q_from * NZ + z_from) * rows, 128), rows)

    own_rows = kv_rows(q, z)
    own = [
        pltpu.make_async_copy(k_hbm.at[:, col(z)], kv.at[0, own_rows, :], loc_sem.at[0]),
        pltpu.make_async_copy(v_hbm.at[:, col(z)], kv.at[1, own_rows, :], loc_sem.at[1]),
        pltpu.make_async_copy(q_hbm.at[:, col(z)], qi.at[z], loc_sem.at[2]),
    ]
    for copy in own:
        copy.start()

    barrier = pltpu.get_barrier_semaphore()

    @pl.loop(1, n_seq)
    def _(offset):
        pl.semaphore_signal(
            barrier,
            inc=1,
            device_id={"seq": (me + offset) % n_seq},
            device_id_type=pl.DeviceIdType.MESH,
        )

    @pl.loop(1, n_dp)
    def _(offset):
        pl.semaphore_signal(
            barrier,
            inc=1,
            device_id={"dp": (dp + offset) % n_dp},
            device_id_type=pl.DeviceIdType.MESH,
        )

    pl.semaphore_wait(barrier, n_seq - 1 + n_dp - 1)

    kvq = {}
    for dz in (2, 1, 3):
        z_to = (z + dz) % NZ
        target = at_z(z_to)
        kvq[dz] = (
            to_seq(k_hbm.at[:, col(z_to)], kv.at[0, own_rows, :], kvq_s.at[0, dz - 1], kvq_r.at[0, dz - 1], target),
            to_seq(v_hbm.at[:, col(z_to)], kv.at[1, own_rows, :], kvq_s.at[1, dz - 1], kvq_r.at[1, dz - 1], target),
            to_seq(q_hbm.at[:, col(z_to)], qi.at[z], kvq_s.at[2, dz - 1], kvq_r.at[2, dz - 1], target),
        )
        kvq[dz][0].start()
        kvq[dz][1].start()
    for dz in (2, 1, 3):
        kvq[dz][2].start()

    lane = lax.broadcasted_iota(jnp.int32, (slots, slots), 1)
    onehot = jnp.where(src_col_ref[...] == lane, 1.0, 0.0).astype(BF16)
    picked = jnp.dot(onehot, states_ref[...], preferred_element_type=F32)
    scaled = (picked * gain_ref[...]).astype(BF16)
    squares = jnp.sum(picked * picked, axis=1, keepdims=True)
    squares_high = squares.astype(BF16)
    squares_low = (squares - squares_high.astype(F32)).astype(BF16)
    tail_lane = lax.broadcasted_iota(jnp.int32, (slots, 128), 1)
    tail = jnp.where(tail_lane < 64, squares_high.astype(F32), squares_low.astype(F32)).astype(BF16)
    load_tp.wait()
    for zz in range(NZ):
        for kind in range(3):
            block = jnp.dot(
                scaled,
                tp[:, kind * inner + zz * hg : kind * inner + (zz + 1) * hg],
                preferred_element_type=F32,
            )
            part[zz, :, kind * hg : (kind + 1) * hg] = block.astype(BF16)
        part[zz, :, 3 * hg : 3 * hg + 128] = tail

    def text_copy(offset):
        target = (me + offset) % n_seq
        z_to = (target // NC) % NZ
        q_to = (target // (NZ * NC)) * NC + target % NC
        return to_seq(
            part.at[z_to, pl.ds(pl.multiple_of(q_to * tq, 32), tq), :],
            tbuf.at[offset - 1],
            txp_s.at[offset - 1],
            txp_r.at[offset - 1],
            target,
        )

    @pl.loop(1, n_seq)
    def _(offset):
        text_copy(offset).start()

    load_dout.wait()
    for t in range(d_model // 128):
        cols = slice(t * 128, (t + 1) * 128)
        gated = gate_ref[:, cols] * dout[:, cols].astype(F32)
        g[:, cols] = gated.astype(BF16)
        gtf[cols, :] = jnp.transpose(gated)
    for p in range(n_dp):
        for qq in range(NQ):
            pieces = []
            for zz in range(NZ):
                owner = (qq // NC) * (NZ * NC) + zz * NC + qq % NC
                start = (p * n_seq + owner) * piece
                pieces.append(gtf[start : start + piece, :])
            gt[qq, p] = jnp.concatenate(pieces, axis=0).astype(BF16)

    def gcols(q_from, z_from):
        return pl.ds(pl.multiple_of((q_from * NZ + z_from) * rows, 128), rows)

    g1 = []
    for i, (q_to, target) in enumerate(((q_y, s_y), (q_c, s_c), (q_d, s_d))):
        copy = to_seq(gt.at[q_to], gt_all.at[:, :, gcols(q, z)], g1_s.at[i], g1_r.at[i], target)
        copy.start()
        g1.append(copy)
    own_g = pltpu.make_async_copy(gt.at[q], gt_all.at[:, :, gcols(q, z)], loc_sem.at[3])
    own_g.start()

    def forward(dz):
        block = kv.at[:, kv_rows(q, (z - dz + NZ) % NZ), :]
        return (
            to_seq(block, block, fwd_s.at[0, dz], fwd_r.at[0, dz], s_y),
            to_seq(block, block, fwd_s.at[1, dz], fwd_r.at[1, dz], s_c),
        )

    def relay(dz):
        block = kv.at[:, kv_rows(q_y, (z - dz + NZ) % NZ), :]
        return to_seq(block, block, fwd_s.at[2, dz], fwd_r.at[2, dz], s_c)

    own[0].wait()
    own[1].wait()
    for dz in (0, 1, 3, 2):
        if dz:
            kvq[dz][0].wait_recv()
            kvq[dz][1].wait_recv()
        for copy in forward(dz):
            copy.start()

    ahead = 1 - 2 * c
    z_p = (z + ahead + NZ) % NZ
    z_n = (z - ahead + NZ) % NZ

    def g_ahead(i, q_from):
        block = gt_all.at[:, :, gcols(q_from, z)]
        return (
            to_seq(block, block, gz_s.at[0, i], gz_r.at[0, i], at_z(z_p)),
            to_seq(block, block, gz_s.at[1, i], gz_r.at[1, i], at_z(z_n)),
        )

    def g_relay(i, q_from):
        block = gt_all.at[:, :, gcols(q_from, z_n)]
        return to_seq(block, block, gz_s.at[2, i], gz_r.at[2, i], at_z(z_p))

    own_g.wait()
    for copy in g_ahead(0, q):
        copy.start()

    load_wo.wait()
    for t in range(inner // 256):
        cols = slice(t * 256, (t + 1) * 256)
        d_attn_ref[:, cols] = jnp.dot(g[...], wo[:, cols], preferred_element_type=F32).astype(BF16)

    for dz in (0, 1, 3, 2):
        forward(dz)[0].wait_recv()
        relay(dz).start()

    def add_part(offset, total):
        text_copy(offset).wait_recv()
        return total + tbuf[offset - 1].astype(F32)

    own_slots = pl.ds(pl.multiple_of(q * tq, 32), tq)
    total = part[z, own_slots, :].astype(F32)
    total = lax.fori_loop(1, n_seq, add_part, total)
    square_sum = total[:, 3 * hg : 3 * hg + 1] + total[:, 3 * hg + 64 : 3 * hg + 65]
    rate = lax.rsqrt(square_sum / (n_seq * states_ref.shape[1]) + EPS)
    normed = total[:, : 3 * hg] * rate
    text_rows = pl.ds(pl.multiple_of(image_keys + q * tq, 32), tq)
    for h in range(n_heads):
        for kind, gains in ((0, qgain_ref), (1, kgain_ref)):
            x = normed[:, kind * hg + h * head : kind * hg + (h + 1) * head]
            x = x * lax.rsqrt(jnp.mean(x * x, axis=1, keepdims=True) + EPS) * gains[...]
            if kind == 0:
                qt[:, h * head : (h + 1) * head] = x.astype(BF16)
            else:
                kv[0, text_rows, h * head : (h + 1) * head] = x.astype(BF16)
    kv[1, text_rows, :] = normed[:, 2 * hg : 3 * hg].astype(BF16)
    text_block = kv.at[:, text_rows, :]
    txkv = []
    for i, target in enumerate((s_y, s_c, s_d)):
        copy = to_seq(text_block, text_block, txkv_s.at[i], txkv_r.at[i], target)
        copy.start()
        txkv.append(copy)

    for i, q_from in ((1, q_y), (2, q_c), (3, q_d)):
        g1[i - 1].wait_recv()
        for copy in g_ahead(i, q_from):
            copy.start()

    own[2].wait()
    for dz in (1, 3, 2):
        kvq[dz][2].wait_recv()
    for dz in (0, 1, 3, 2):
        forward(dz)[1].wait_recv()
        relay(dz).wait_recv()
    for copy in txkv:
        copy.wait_recv()

    factor = head ** (-0.5) * math.log2(math.e)
    bias = jnp.where(src_row_ref[...] < clen_ref[0], 0.0, NEG_BIG)

    def attend(query, h):
        cols = slice(h * head, (h + 1) * head)
        image_scores = lax.dot_general(query, kv[0, :image_keys, cols], NT, preferred_element_type=F32)
        text_scores = lax.dot_general(query, kv[0, image_keys:, cols], NT, preferred_element_type=F32) + bias
        top = jnp.maximum(
            jnp.max(image_scores, axis=1, keepdims=True), jnp.max(text_scores, axis=1, keepdims=True)
        )
        image_probs = jnp.exp2((image_scores - top) * factor)
        text_probs = jnp.exp2((text_scores - top) * factor)
        denom = jnp.sum(image_probs, axis=1, keepdims=True) + jnp.sum(text_probs, axis=1, keepdims=True)
        summed = jnp.dot(image_probs.astype(BF16), kv[1, :image_keys, cols], preferred_element_type=F32)
        summed += jnp.dot(text_probs.astype(BF16), kv[1, image_keys:, cols], preferred_element_type=F32)
        return summed / denom

    def a_block(q_from, z_of):
        return a_all.at[kv_rows(q_from, z_of), :]

    def a_return(i):
        z_to = (z + i + 1) % NZ
        return to_seq(a_block(q, z_to), a_rows.at[z], aret_s.at[i], aret_r.at[i], at_z(z_to))

    def a_plane(i):
        block = a_block(q, (z + i + 1) % NZ)
        return (
            to_seq(block, block, apl_s.at[0, i], apl_r.at[0, i], s_y),
            to_seq(block, block, apl_s.at[1, i], apl_r.at[1, i], s_c),
        )

    def a_relay(i):
        block = a_block(q_y, (z + i + 1) % NZ)
        return to_seq(block, block, apl_s.at[2, i], apl_r.at[2, i], s_c)

    def g_source(i):
        y_from = (y + i % 2) % NY
        c_from = (c + i // 2) % NC
        return y_from * NC + c_from

    @pl.loop(0, NZ)
    def _(i):
        z_to = (z + i + 1) % NZ
        for h in range(n_heads):
            cols = slice(h * head, (h + 1) * head)
            result = attend(qi[z_to, :, cols], h)
            a_all[kv_rows(q, z_to), cols] = result.astype(BF16)

        @pl.when(i < NZ - 1)
        def _():
            a_return(i).start()

        for copy in a_plane(i):
            copy.start()
        source = g_source(i)
        g_ahead(i, source)[0].wait_recv()
        g_relay(i, source).start()

    a_rows[z] = a_all[kv_rows(q, z), :]

    slot_valid = src_col_ref[own_slots, :] < clen_ref[0]
    for h in range(n_heads):
        cols = slice(h * head, (h + 1) * head)
        result = jnp.where(slot_valid, attend(qt[:, cols], h), 0.0)
        for zz in range(NZ):
            tsend[zz, :, cols] = result[zz * ts : (zz + 1) * ts, :]

    def t_return(dz):
        z_to = (z + dz) % NZ
        return to_seq(tsend.at[z_to], trecv.at[z], tret_s.at[dz - 1], tret_r.at[dz - 1], at_z(z_to))

    for dz in range(1, NZ):
        t_return(dz).start()
    trecv[z] = tsend[z]

    @pl.loop(0, NZ)
    def _(i):
        a_plane(i)[0].wait_recv()
        a_relay(i).start()

    @pl.loop(0, NZ)
    def _(i):
        source = g_source(i)
        g_ahead(i, source)[1].wait_recv()
        g_relay(i, source).wait_recv()
        a_plane(i)[1].wait_recv()

    @pl.loop(0, NZ)
    def _(i):
        a_relay(i).wait_recv()

    def grad_block(p):
        return jnp.dot(gt_all[p], a_all[...], preferred_element_type=F32)

    def dp_copy(j):
        p = (dp + 1 + j) % n_dp
        return pltpu.make_async_remote_copy(
            src_ref=psend.at[p],
            dst_ref=precv.at[j],
            send_sem=dp_s.at[j],
            recv_sem=dp_r.at[j],
            device_id={"dp": p},
            device_id_type=pl.DeviceIdType.MESH,
        )

    @pl.loop(0, n_dp - 1)
    def _(j):
        p = (dp + 1 + j) % n_dp
        psend[p] = grad_block(p).astype(BF16)
        dp_copy(j).start()

    own_grad = grad_block(dp)

    for i in range(NZ - 1):
        a_return(i).wait_recv()
    image_attn = jnp.concatenate([a_rows[zz] for zz in range(NZ)], axis=1)
    per = d_model // n_seq
    for t in range(n_seq // 2):
        cols = slice(t * 2 * per, (t + 1) * 2 * per)
        projected = lax.dot_general(image_attn, wo[cols, :], NT, preferred_element_type=F32)
        image_out_ref[:, cols] = (gate_ref[:, cols] * projected).astype(BF16)
        term = jnp.sum(projected * dout[:, cols].astype(F32), axis=0, keepdims=True)
        gsend[2 * t, :, :per] = jnp.broadcast_to(term[:, :per], (8, per))
        gsend[2 * t + 1, :, :per] = jnp.broadcast_to(term[:, per:], (8, per))

    def gate_copy(offset):
        target = (me + offset) % n_seq
        return to_seq(gsend.at[target], grecv.at[offset - 1], gg_s.at[offset - 1], gg_r.at[offset - 1], target)

    @pl.loop(1, n_seq)
    def _(offset):
        gate_copy(offset).start()

    def add_grad(j, total):
        dp_copy(j).wait_recv()
        return total + precv[j].astype(F32)

    grad = lax.fori_loop(0, n_dp - 1, add_grad, own_grad)
    for zz in range(NZ):
        fsend[zz] = grad[zz * piece : (zz + 1) * piece, :]

    def final_copy(dz):
        z_to = (z + dz) % NZ
        return to_seq(fsend.at[z_to], fin.at[z], fin_s.at[dz - 1], fin_r.at[dz - 1], at_z(z_to))

    for dz in range(1, NZ):
        final_copy(dz).start()
    fin[z] = fsend[z]

    for dz in range(1, NZ):
        t_return(dz).wait_recv()
    for zz in range(NZ):
        text_attn_ref[:, zz * hg : (zz + 1) * hg] = trecv[zz].astype(BF16)

    def add_gate(offset, total):
        gate_copy(offset).wait_recv()
        return total + grecv[offset - 1]

    gate_total = lax.fori_loop(1, n_seq, add_gate, gsend[me])
    grad_gate_ref[...] = gate_total[0:1, :per]

    for dz in range(1, NZ):
        final_copy(dz).wait_recv()
    for zz in range(NZ):
        grad_wo_ref[:, zz * hg : (zz + 1) * hg] = fin[zz]

    for dz in range(1, NZ):
        for copy in kvq[dz]:
            copy.wait_send()
        t_return(dz).wait_send()
        final_copy(dz).wait_send()
        a_return(dz - 1).wait_send()
    for copy in g1 + txkv:
        copy.wait_send()

    @pl.loop(0, NZ)
    def _(i):
        source = g_source(i)
        for copy in (*forward(i), relay(i), *g_ahead(i, source), g_relay(i, source), *a_plane(i), a_relay(i)):
            copy.wait_send()

    @pl.loop(1, n_seq)
    def _(offset):
        text_copy(offset).wait_send()
        gate_copy(offset).wait_send()

    @pl.loop(0, n_dp - 1)
    def _(j):
        dp_copy(j).wait_send()


def on_device(
    n_dp,
    caption_states,
    caption_gain,
    text_proj,
    caption_len,
    slot_source,
    query_gain,
    key_gain,
    image_q,
    image_k,
    image_v,
    out_weight,
    gate,
    d_out,
):
    slots = slot_source.shape[1]
    rows, inner = image_q.shape[1:]
    d_model = d_out.shape[2]
    n_seq = NY * NZ * NC
    hg = inner // NZ
    tq = slots // NQ
    ts = tq // NZ
    blk = d_model // n_dp // NQ
    piece = blk // NZ
    per = d_model // n_seq
    sources = slot_source[0].reshape(NY, NZ, NC, ts).transpose(0, 2, 1, 3).reshape(slots)
    vmem = pl.BlockSpec(memory_space=pltpu.VMEM)
    hbm = pl.BlockSpec(memory_space=pl.ANY)
    smem = pl.BlockSpec(memory_space=pltpu.SMEM)
    dma = pltpu.SemaphoreType.DMA
    sems = [
        (3,), (4,), (3, 3), (3, 3), (3, NZ), (3, NZ), (n_seq - 1,), (n_seq - 1,), (3,), (3,), (3,), (3,),
        (3, NZ), (3, NZ), (3,), (3,), (3,), (3,), (3, NZ), (3, NZ), (n_dp - 1,), (n_dp - 1,), (3,), (3,),
        (n_seq - 1,), (n_seq - 1,),
    ]
    outs = pl.pallas_call(
        functools.partial(joint_kernel, n_dp),
        out_shape=(
            jax.ShapeDtypeStruct((rows, d_model), BF16),
            jax.ShapeDtypeStruct((ts, inner), BF16),
            jax.ShapeDtypeStruct((rows, inner), BF16),
            jax.ShapeDtypeStruct((piece, inner), F32),
            jax.ShapeDtypeStruct((1, per), F32),
        ),
        in_specs=[vmem, vmem, hbm, vmem, vmem, smem, vmem, vmem, hbm, hbm, hbm, hbm, vmem, hbm],
        out_specs=(vmem,) * 5,
        scratch_shapes=[
            pltpu.VMEM(text_proj.shape, BF16),
            pltpu.VMEM(out_weight.shape, BF16),
            pltpu.VMEM((rows, d_model), BF16),
            pltpu.VMEM((NZ, slots, 3 * hg + 128), BF16),
            pltpu.VMEM((n_seq - 1, tq, 3 * hg + 128), BF16),
            pltpu.VMEM((NZ, rows, hg), BF16),
            pltpu.VMEM((tq, hg), BF16),
            pltpu.VMEM((2, n_seq * rows + slots, hg), BF16),
            pltpu.VMEM((rows, d_model), BF16),
            pltpu.VMEM((d_model, rows), F32),
            pltpu.VMEM((NQ, n_dp, blk, rows), BF16),
            pltpu.VMEM((n_dp, blk, n_seq * rows), BF16),
            pltpu.VMEM((n_seq * rows, hg), BF16),
            pltpu.VMEM((NZ, rows, hg), BF16),
            pltpu.VMEM((NZ, ts, hg), F32),
            pltpu.VMEM((NZ, ts, hg), F32),
            pltpu.VMEM((n_dp, blk, hg), BF16),
            pltpu.VMEM((n_dp - 1, blk, hg), BF16),
            pltpu.VMEM((NZ, piece, hg), F32),
            pltpu.VMEM((NZ, piece, hg), F32),
            pltpu.VMEM((n_seq, 8, 256), F32),
            pltpu.VMEM((n_seq - 1, 8, 256), F32),
            *[dma(shape) for shape in sems],
        ],
        compiler_params=pltpu.CompilerParams(
            collective_id=0, has_side_effects=True, vmem_limit_bytes=58 * 1024 * 1024
        ),
        name="joint",
    )(
        caption_states[0],
        caption_gain[None],
        text_proj,
        sources[:, None],
        sources[None],
        caption_len,
        query_gain[None],
        key_gain[None],
        image_q[0],
        image_k[0],
        image_v[0],
        out_weight,
        gate,
        d_out[0],
    )
    image_out, text_attn, d_attn, grad_wo, grad_gate = outs
    return (image_out[None], text_attn[None], d_attn[None], grad_wo, grad_gate)


def solution(mesh):
    in_specs = (
        P("dp", None, "seq"),
        P("seq"),
        P("seq", None),
        P("dp"),
        P("dp", None),
        P(),
        P(),
        P("dp", "seq", None),
        P("dp", "seq", None),
        P("dp", "seq", None),
        P(),
        P("dp", None),
        P("dp", "seq", None),
    )
    out_specs = (
        P("dp", "seq", None),
        P("dp", "seq", None),
        P("dp", "seq", None),
        P(("dp", "seq"), None),
        P("dp", "seq"),
    )
    return jax.shard_map(
        functools.partial(on_device, mesh.shape["dp"]),
        mesh=mesh,
        in_specs=in_specs,
        out_specs=out_specs,
        check_vma=False,
    )
```

```python
import functools
import math

import jax
import jax.numpy as jnp
from jax import lax
from jax.experimental import pallas as pl
from jax.experimental.pallas import tpu as pltpu
from jax.sharding import PartitionSpec as P

EPS = 1e-06
NEG_BIG = -1e30
NY, NZ, NC = 2, 4, 2
NQ = NY * NC
F32 = jnp.float32
BF16 = jnp.bfloat16
NT = (((1,), (1,)), ((), ()))


def joint_kernel(
    n_dp,
    states_ref,
    gain_ref,
    text_proj_hbm,
    source_ref,
    length_ref,
    qgain_ref,
    kgain_ref,
    q_hbm,
    k_hbm,
    v_hbm,
    wo_hbm,
    gate_ref,
    dout_hbm,
    image_out_ref,
    text_attn_ref,
    d_attn_ref,
    grad_wo_ref,
    grad_gate_ref,
    tp,
    wo,
    dout,
    part,
    core_recv,
    ysend_q,
    ysend_kv,
    yrecv_q,
    yrecv_kv,
    zsend_q,
    zsend_kv,
    zrecv_q,
    zrecv_kv,
    sq_send,
    sq_recv,
    sq_col,
    src_col,
    qi,
    qt,
    near_top,
    near_sum,
    near_acc,
    kv,
    g,
    gtf,
    gt,
    gt_all,
    a_all,
    a_rows,
    tsend,
    trecv,
    psend,
    precv,
    own_grad,
    fin,
    gsend,
    grecv,
    load_sem,
    loc_sem,
    kvq_s,
    kvq_r,
    fwd_s,
    fwd_r,
    core_s,
    core_r,
    ytx_s,
    ytx_r,
    ztx_s,
    ztx_r,
    sq_s,
    sq_r,
    txkv_s,
    txkv_r,
    g1_s,
    g1_r,
    gz_s,
    gz_r,
    aret_s,
    aret_r,
    tret_s,
    tret_r,
    apl_s,
    apl_r,
    dp_s,
    dp_r,
    gg_s,
    gg_r,
):
    dp = lax.axis_index("dp")
    me = lax.axis_index("seq")
    n_seq = NY * NZ * NC
    y = me // (NZ * NC)
    z = (me // NC) % NZ
    c = me % NC
    q = y * NC + c
    rows, inner = a_rows.shape[1], NZ * a_rows.shape[2]
    hg = a_rows.shape[2]
    head = 128
    n_heads = hg // head
    d_model = dout.shape[1]
    slots = source_ref.shape[1]
    tq = slots // NQ
    ts = tq // NZ
    image_keys = n_seq * rows
    blk = gt.shape[2]
    piece = blk // NZ

    def at_z(z_to):
        return y * (NZ * NC) + z_to * NC + c

    s_y = (1 - y) * (NZ * NC) + z * NC + c
    s_c = y * (NZ * NC) + z * NC + (1 - c)
    s_d = (1 - y) * (NZ * NC) + z * NC + (1 - c)
    q_y = (1 - y) * NC + c
    q_c = y * NC + (1 - c)
    q_d = (1 - y) * NC + (1 - c)

    def to_seq(src, dst, ss, rs, target):
        return pltpu.make_async_remote_copy(
            src_ref=src,
            dst_ref=dst,
            send_sem=ss,
            recv_sem=rs,
            device_id={"seq": target},
            device_id_type=pl.DeviceIdType.MESH,
        )

    load_tp = pltpu.make_async_copy(text_proj_hbm, tp, load_sem.at[0])
    load_dout = pltpu.make_async_copy(dout_hbm, dout, load_sem.at[1])
    load_wo = pltpu.make_async_copy(wo_hbm, wo, load_sem.at[2])
    load_tp.start()
    load_dout.start()
    load_wo.start()

    def col(index):
        return pl.ds(pl.multiple_of(index * hg, 128), hg)

    def kv_rows(q_from, z_from):
        return pl.ds(pl.multiple_of((q_from * NZ + z_from) * rows, 128), rows)

    own_rows = kv_rows(q, z)
    own = [
        pltpu.make_async_copy(k_hbm.at[:, col(z)], kv.at[0, own_rows, :], loc_sem.at[0]),
        pltpu.make_async_copy(v_hbm.at[:, col(z)], kv.at[1, own_rows, :], loc_sem.at[1]),
        pltpu.make_async_copy(q_hbm.at[:, col(z)], qi.at[z], loc_sem.at[2]),
    ]
    for copy in own:
        copy.start()

    barrier = pltpu.get_barrier_semaphore()

    @pl.loop(1, n_seq)
    def _(offset):
        pl.semaphore_signal(
            barrier,
            inc=1,
            device_id={"seq": (me + offset) % n_seq},
            device_id_type=pl.DeviceIdType.MESH,
        )

    @pl.loop(1, n_dp)
    def _(offset):
        for z_to in range(NZ):
            pl.semaphore_signal(
                barrier,
                inc=1,
                device_id={"dp": (dp + offset) % n_dp, "seq": at_z(z_to)},
                device_id_type=pl.DeviceIdType.MESH,
            )

    pl.semaphore_wait(barrier, n_seq - 1 + NZ * (n_dp - 1))

    kvq = {}
    for dz in (2, 1, 3):
        z_to = (z + dz) % NZ
        target = at_z(z_to)
        kvq[dz] = (
            to_seq(k_hbm.at[:, col(z_to)], kv.at[0, own_rows, :], kvq_s.at[0, dz - 1], kvq_r.at[0, dz - 1], target),
            to_seq(v_hbm.at[:, col(z_to)], kv.at[1, own_rows, :], kvq_s.at[1, dz - 1], kvq_r.at[1, dz - 1], target),
            to_seq(q_hbm.at[:, col(z_to)], qi.at[z], kvq_s.at[2, dz - 1], kvq_r.at[2, dz - 1], target),
        )
        kvq[dz][0].start()
        kvq[dz][1].start()
    for dz in (2, 1, 3):
        kvq[dz][2].start()

    def forward(dz):
        block = kv.at[:, kv_rows(q, (z - dz + NZ) % NZ), :]
        return (
            to_seq(block, block, fwd_s.at[0, dz], fwd_r.at[0, dz], s_y),
            to_seq(block, block, fwd_s.at[1, dz], fwd_r.at[1, dz], s_c),
        )

    def relay(dz):
        block = kv.at[:, kv_rows(q_y, (z - dz + NZ) % NZ), :]
        return to_seq(block, block, fwd_s.at[2, dz], fwd_r.at[2, dz], s_c)

    own[0].wait()
    own[1].wait()
    for copy in forward(0):
        copy.start()

    place = lax.broadcasted_iota(jnp.int32, (slots, slots), 0)
    lane = lax.broadcasted_iota(jnp.int32, (slots, slots), 1)
    at_c, at_y = place // (slots // NC), (place // tq) % NY
    slot_of = at_y * (slots // NY) + ((place // ts) % NZ) * (NC * ts) + at_c * ts + place % ts
    order = jnp.where(lane == slot_of, 1.0, 0.0).astype(BF16)
    row_at_slot = jnp.where(place == source_ref[...], 1.0, 0.0).astype(BF16)
    onehot = lax.dot_general(order, row_at_slot, NT, preferred_element_type=F32)
    src_col[...] = jnp.broadcast_to(
        jnp.sum(onehot * lane.astype(F32), axis=1, keepdims=True), (slots, slots)
    )
    onehot = onehot.astype(BF16)
    src_row = lax.dot_general(lane[:8].astype(F32).astype(BF16), onehot, NT, preferred_element_type=F32)
    picked = jnp.dot(onehot, states_ref[...], preferred_element_type=F32)
    scaled = (picked * gain_ref[...]).astype(BF16)
    squares = jnp.sum(picked * picked, axis=1, keepdims=True)
    sq_send[...] = jnp.transpose(jnp.broadcast_to(squares, (slots, slots)))[:8]

    load_tp.wait()
    for zz in range(NZ):
        for kind in range(3):
            block = jnp.dot(
                scaled,
                tp[:, kind * inner + zz * hg : kind * inner + (zz + 1) * hg],
                preferred_element_type=F32,
            )
            for i in range(NQ):
                part[i // NY, i % NY, zz, :, kind * hg : (kind + 1) * hg] = block[i * tq : (i + 1) * tq]

    core_copy = to_seq(part.at[1 - c], core_recv, core_s.at[0], core_r.at[0], s_c)
    core_copy.start()

    def square_copy(offset):
        target = (me + offset) % n_seq
        return to_seq(sq_send, sq_recv.at[offset - 1], sq_s.at[offset - 1], sq_r.at[offset - 1], target)

    @pl.loop(1, n_seq)
    def _(offset):
        square_copy(offset).start()

    load_dout.wait()
    for t in range(d_model // 128):
        cols = slice(t * 128, (t + 1) * 128)
        gated = gate_ref[:, cols] * dout[:, cols].astype(F32)
        g[:, cols] = gated.astype(BF16)
        gtf[cols, :] = jnp.transpose(gated)

    core_copy.wait_recv()
    for zz in range(NZ):
        summed = part[c, 1 - y, zz] + core_recv[1 - y, zz]
        ysend_q[zz] = summed[:, :hg]
        ysend_kv[zz] = summed[:, hg:].astype(BF16)
    y_copies = (
        to_seq(ysend_q, yrecv_q, ytx_s.at[0], ytx_r.at[0], s_y),
        to_seq(ysend_kv, yrecv_kv, ytx_s.at[1], ytx_r.at[1], s_y),
    )
    for copy in y_copies:
        copy.start()

    for p in range(n_dp):
        for qq in range(NQ):
            pieces = []
            for zz in range(NZ):
                owner = (qq // NC) * (NZ * NC) + zz * NC + qq % NC
                start = (p * n_seq + owner) * piece
                pieces.append(gtf[start : start + piece, :])
            gt[qq, p] = jnp.concatenate(pieces, axis=0).astype(BF16)

    def gcols(q_from, z_from):
        return pl.ds(pl.multiple_of((q_from * NZ + z_from) * rows, 128), rows)

    g1 = [
        to_seq(gt.at[q_to], gt_all.at[:, :, gcols(q, z)], g1_s.at[i], g1_r.at[i], target)
        for i, (q_to, target) in enumerate(((q_y, s_y), (q_c, s_c), (q_d, s_d)))
    ]
    g1[1].start()
    own_g = pltpu.make_async_copy(gt.at[q], gt_all.at[:, :, gcols(q, z)], loc_sem.at[3])
    own_g.start()

    ahead = 1 - 2 * c
    z_p = (z + ahead + NZ) % NZ
    z_n = (z - ahead + NZ) % NZ

    def g_ahead(i, q_from):
        block = gt_all.at[:, :, gcols(q_from, z)]
        return (
            to_seq(block, block, gz_s.at[0, i], gz_r.at[0, i], at_z(z_p)),
            to_seq(block, block, gz_s.at[1, i], gz_r.at[1, i], at_z(z_n)),
        )

    def g_relay(i, q_from):
        block = gt_all.at[:, :, gcols(q_from, z_n)]
        return to_seq(block, block, gz_s.at[2, i], gz_r.at[2, i], at_z(z_p))

    load_wo.wait()
    for t in range(inner // 256):
        cols = slice(t * 256, (t + 1) * 256)
        d_attn_ref[:, cols] = jnp.dot(g[...], wo[:, cols], preferred_element_type=F32).astype(BF16)

    for dz in (1, 3, 2):
        kvq[dz][0].wait_recv()
        kvq[dz][1].wait_recv()
        for copy in forward(dz):
            copy.start()

    for copy in y_copies:
        copy.wait_recv()
    for zz in range(NZ):
        summed = part[c, y, zz] + core_recv[y, zz]
        zsend_q[zz] = summed[:, :hg] + yrecv_q[zz]
        part[c, y, zz, :, hg:] = summed[:, hg:] + yrecv_kv[zz].astype(F32)
        zsend_kv[zz] = part[c, y, zz, :, hg:].astype(BF16)

    z_copies = []
    for dz in (2, 1, 3):
        z_to = (z + dz) % NZ
        for kind, (src, dst) in enumerate(((zsend_q, zrecv_q), (zsend_kv, zrecv_kv))):
            copy = to_seq(
                src.at[z_to], dst.at[dz - 1], ztx_s.at[kind, dz - 1], ztx_r.at[kind, dz - 1], at_z(z_to)
            )
            copy.start()
            z_copies.append(copy)

    own_g.wait()
    for copy in g_ahead(0, q):
        copy.start()
    g1[1].wait_recv()
    for copy in g_ahead(2, q_c):
        copy.start()

    own[2].wait()
    for dz in (1, 3, 2):
        kvq[dz][2].wait_recv()
    for dz in (0, 1, 3, 2):
        forward(dz)[1].wait_recv()

    factor = head ** (-0.5) * math.log2(math.e)
    half = image_keys // NY
    near_rows = pl.ds(pl.multiple_of(y * half, 128), half)
    far_rows = pl.ds(pl.multiple_of((1 - y) * half, 128), half)

    def attend_near(query, h):
        cols = slice(h * head, (h + 1) * head)
        scores = lax.dot_general(query, kv[0, near_rows, cols], NT, preferred_element_type=F32)
        top = jnp.max(scores, axis=1, keepdims=True)
        probs = jnp.exp2((scores - top) * factor)
        values = jnp.dot(probs.astype(BF16), kv[1, near_rows, cols], preferred_element_type=F32)
        return top, jnp.sum(probs, axis=1, keepdims=True), values

    for i in range(NZ):
        z_to = (z + i + 1) % NZ
        for h in range(n_heads):
            cols = slice(h * head, (h + 1) * head)
            top, total, values = attend_near(qi[z_to, :, cols], h)
            near_top[i, h] = jnp.broadcast_to(top, (rows, head))
            near_sum[i, h] = jnp.broadcast_to(total, (rows, head))
            near_acc[i, :, cols] = values
        dz = (0, 1, 3, 2)[i]
        forward(dz)[0].wait_recv()
        relay(dz).start()
        if i == 1:
            g1[0].start()
            g1[2].start()

    def add_square(offset, total):
        square_copy(offset).wait_recv()
        return total + sq_recv[offset - 1]

    square_row = lax.fori_loop(1, n_seq, add_square, sq_send[...])
    sq_col[...] = jnp.transpose(jnp.broadcast_to(square_row[0:1], (slots, slots)))
    own_slots = pl.ds(pl.multiple_of((c * NY + y) * tq, 32), tq)
    rate = lax.rsqrt(sq_col[own_slots, 0:1] / (n_seq * states_ref.shape[1]) + EPS)
    for copy in z_copies:
        copy.wait_recv()
    total_q = zsend_q[z]
    total_kv = part[c, y, z, :, hg:]
    for dz in range(1, NZ):
        total_q += zrecv_q[dz - 1]
        total_kv += zrecv_kv[dz - 1].astype(F32)
    normed_q, normed_kv = total_q * rate, total_kv * rate
    text_rows = pl.ds(pl.multiple_of(image_keys + (c * NY + y) * tq, 32), tq)
    for h in range(n_heads):
        cols = slice(h * head, (h + 1) * head)
        x = normed_q[:, cols]
        qt[:, cols] = (x * lax.rsqrt(jnp.mean(x * x, axis=1, keepdims=True) + EPS) * qgain_ref[...]).astype(BF16)
        x = normed_kv[:, cols]
        kv[0, text_rows, cols] = (
            x * lax.rsqrt(jnp.mean(x * x, axis=1, keepdims=True) + EPS) * kgain_ref[...]
        ).astype(BF16)
    kv[1, text_rows, :] = normed_kv[:, hg:].astype(BF16)
    text_block = kv.at[:, text_rows, :]
    txkv = []
    for i, target in enumerate((s_y, s_c, s_d)):
        copy = to_seq(text_block, text_block, txkv_s.at[i], txkv_r.at[i], target)
        copy.start()
        txkv.append(copy)

    for i, q_from in ((1, q_y), (3, q_d)):
        g1[i - 1].wait_recv()
        for copy in g_ahead(i, q_from):
            copy.start()
    for dz in (0, 1, 3, 2):
        relay(dz).wait_recv()
    for copy in txkv:
        copy.wait_recv()

    length = length_ref[...].astype(F32)
    bias = jnp.where(src_row[0:1] < length, 0.0, NEG_BIG)

    def attend(query, h, near):
        cols = slice(h * head, (h + 1) * head)
        near_max, near_total, near_values = near
        image_scores = lax.dot_general(query, kv[0, far_rows, cols], NT, preferred_element_type=F32)
        text_scores = lax.dot_general(query, kv[0, image_keys:, cols], NT, preferred_element_type=F32) + bias
        top = jnp.maximum(
            jnp.max(image_scores, axis=1, keepdims=True), jnp.max(text_scores, axis=1, keepdims=True)
        )
        top = jnp.maximum(top, near_max)
        image_probs = jnp.exp2((image_scores - top) * factor)
        text_probs = jnp.exp2((text_scores - top) * factor)
        scale = jnp.exp2((near_max - top) * factor)
        denom = jnp.sum(image_probs, axis=1, keepdims=True) + jnp.sum(text_probs, axis=1, keepdims=True)
        summed = jnp.dot(image_probs.astype(BF16), kv[1, far_rows, cols], preferred_element_type=F32)
        summed += jnp.dot(text_probs.astype(BF16), kv[1, image_keys:, cols], preferred_element_type=F32)
        return (summed + scale * near_values) / (denom + scale * near_total)

    def a_block(q_from, z_of):
        return a_all.at[kv_rows(q_from, z_of), :]

    def a_return(i):
        z_to = (z + i + 1) % NZ
        return to_seq(a_block(q, z_to), a_rows.at[z], aret_s.at[i], aret_r.at[i], at_z(z_to))

    def a_plane(i):
        block = a_block(q, (z + i + 1) % NZ)
        return (
            to_seq(block, block, apl_s.at[0, i], apl_r.at[0, i], s_y),
            to_seq(block, block, apl_s.at[1, i], apl_r.at[1, i], s_c),
        )

    def a_relay(i):
        block = a_block(q_y, (z + i + 1) % NZ)
        return to_seq(block, block, apl_s.at[2, i], apl_r.at[2, i], s_c)

    def g_source(i):
        y_from = (y + i % 2) % NY
        c_from = (c + i // 2) % NC
        return y_from * NC + c_from

    @pl.loop(0, NZ)
    def _(i):
        z_to = (z + i + 1) % NZ
        for h in range(n_heads):
            cols = slice(h * head, (h + 1) * head)
            near = near_top[i, h][:, :1], near_sum[i, h][:, :1], near_acc[i, :, cols]
            result = attend(qi[z_to, :, cols], h, near)
            a_all[kv_rows(q, z_to), cols] = result.astype(BF16)

        @pl.when(i < NZ - 1)
        def _():
            a_return(i).start()

        for copy in a_plane(i):
            copy.start()
        k = (i % 2) * 2 + i // 2
        source = g_source(k)
        g_ahead(k, source)[0].wait_recv()
        g_relay(k, source).start()

        @pl.when(i > 0)
        def _():
            a_plane(i - 1)[0].wait_recv()
            a_relay(i - 1).start()

    a_rows[z] = a_all[kv_rows(q, z), :]

    slot_valid = src_col[own_slots, 0:1] < length
    for h in range(n_heads):
        cols = slice(h * head, (h + 1) * head)
        result = jnp.where(slot_valid, attend(qt[:, cols], h, attend_near(qt[:, cols], h)), 0.0)
        for zz in range(NZ):
            tsend[zz, :, cols] = result[zz * ts : (zz + 1) * ts, :]

    def t_return(dz):
        z_to = (z + dz) % NZ
        return to_seq(tsend.at[z_to], trecv.at[z], tret_s.at[dz - 1], tret_r.at[dz - 1], at_z(z_to))

    for dz in range(1, NZ):
        t_return(dz).start()
    trecv[z] = tsend[z]

    a_plane(NZ - 1)[0].wait_recv()
    a_relay(NZ - 1).start()

    for i in range(NZ - 1):
        a_return(i).wait_recv()
    image_attn = jnp.concatenate([a_rows[zz] for zz in range(NZ)], axis=1)
    per = d_model // n_seq
    for t in range(n_seq // 2):
        cols = slice(t * 2 * per, (t + 1) * 2 * per)
        projected = lax.dot_general(image_attn, wo[cols, :], NT, preferred_element_type=F32)
        image_out_ref[:, cols] = (gate_ref[:, cols] * projected).astype(BF16)
        term = jnp.sum(projected * dout[:, cols].astype(F32), axis=0, keepdims=True)
        gsend[2 * t, :, :per] = jnp.broadcast_to(term[:, :per], (8, per))
        gsend[2 * t + 1, :, :per] = jnp.broadcast_to(term[:, per:], (8, per))

    def gate_copy(offset):
        target = (me + offset) % n_seq
        return to_seq(gsend.at[target], grecv.at[offset - 1], gg_s.at[offset - 1], gg_r.at[offset - 1], target)

    @pl.loop(1, n_seq)
    def _(offset):
        gate_copy(offset).start()

    @pl.loop(0, NZ)
    def _(i):
        source = g_source(i)
        g_ahead(i, source)[1].wait_recv()
        g_relay(i, source).wait_recv()
        a_plane(i)[1].wait_recv()
        a_relay(i).wait_recv()

    def grad_block(p):
        return jnp.dot(gt_all[p], a_all[...], preferred_element_type=F32)

    def dp_copy(jd, jz):
        p, z_to = (dp + jd) % n_dp, (z + jz) % NZ
        return pltpu.make_async_remote_copy(
            src_ref=psend.at[p, z_to],
            dst_ref=precv.at[jd, jz],
            send_sem=dp_s.at[jd, jz],
            recv_sem=dp_r.at[jd, jz],
            device_id={"dp": p, "seq": at_z(z_to)},
            device_id_type=pl.DeviceIdType.MESH,
        )

    @pl.loop(1, n_dp)
    def _(jd):
        p = (dp + jd) % n_dp
        block = grad_block(p)
        for zz in range(NZ):
            psend[p, zz] = block[zz * piece : (zz + 1) * piece].astype(BF16)
        for jz in range(NZ):
            dp_copy(jd, jz).start()

    block = grad_block(dp)
    for zz in range(NZ):
        own_grad[zz] = block[zz * piece : (zz + 1) * piece]
        psend[dp, zz] = block[zz * piece : (zz + 1) * piece].astype(BF16)
    for jz in range(1, NZ):
        dp_copy(0, jz).start()

    for dz in range(1, NZ):
        t_return(dz).wait_recv()
    for zz in range(NZ):
        text_attn_ref[:, zz * hg : (zz + 1) * hg] = trecv[zz].astype(BF16)

    def add_gate(offset, total):
        gate_copy(offset).wait_recv()
        return total + grecv[offset - 1]

    gate_total = lax.fori_loop(1, n_seq, add_gate, gsend[me])
    grad_gate_ref[...] = gate_total[0:1, :per]

    for jz in range(NZ):
        if jz:
            dp_copy(0, jz).wait_recv()
            first = precv[0, jz].astype(F32)
        else:
            first = own_grad[z]

        def add_grad(jd, total):
            dp_copy(jd, jz).wait_recv()
            return total + precv[jd, jz].astype(F32)

        fin[(z - jz + NZ) % NZ] = lax.fori_loop(1, n_dp, add_grad, first)
    for zz in range(NZ):
        grad_wo_ref[:, zz * hg : (zz + 1) * hg] = fin[zz]

    for dz in range(1, NZ):
        for copy in kvq[dz]:
            copy.wait_send()
        t_return(dz).wait_send()
        a_return(dz - 1).wait_send()
        dp_copy(0, dz).wait_send()
    for copy in (*g1, *txkv, *y_copies, *z_copies, core_copy):
        copy.wait_send()

    @pl.loop(0, NZ)
    def _(i):
        source = g_source(i)
        for copy in (*forward(i), relay(i), *g_ahead(i, source), g_relay(i, source), *a_plane(i), a_relay(i)):
            copy.wait_send()

    @pl.loop(1, n_seq)
    def _(offset):
        square_copy(offset).wait_send()
        gate_copy(offset).wait_send()

    @pl.loop(1, n_dp)
    def _(jd):
        for jz in range(NZ):
            dp_copy(jd, jz).wait_send()


def copy_out(*refs):
    sources, results, sem = refs[:5], refs[5:10], refs[10]
    copies = [
        pltpu.make_async_copy(src, dst, sem.at[i]) for i, (src, dst) in enumerate(zip(sources, results))
    ]
    for copy in copies:
        copy.start()
    for copy in copies:
        copy.wait()


def on_device(
    n_dp,
    caption_states,
    caption_gain,
    text_proj,
    caption_len,
    slot_source,
    query_gain,
    key_gain,
    image_q,
    image_k,
    image_v,
    out_weight,
    gate,
    d_out,
):
    slots = slot_source.shape[1]
    rows, inner = image_q.shape[1:]
    d_model = d_out.shape[2]
    n_seq = NY * NZ * NC
    hg = inner // NZ
    tq = slots // NQ
    ts = tq // NZ
    blk = d_model // n_dp // NQ
    piece = blk // NZ
    per = d_model // n_seq
    vmem = pl.BlockSpec(memory_space=pltpu.VMEM)
    hbm = pl.BlockSpec(memory_space=pl.ANY)
    dma = pltpu.SemaphoreType.DMA
    sems = [
        (3,), (4,), (3, 3), (3, 3), (3, NZ), (3, NZ), (1,), (1,), (2,), (2,), (2, 3), (2, 3), (n_seq - 1,),
        (n_seq - 1,), (3,), (3,), (3,), (3,), (3, NZ), (3, NZ), (3,), (3,), (3,), (3,), (3, NZ), (3, NZ),
        (n_dp, NZ), (n_dp, NZ), (n_seq - 1,), (n_seq - 1,),
    ]
    out_shape = (
        jax.ShapeDtypeStruct((rows, d_model), BF16),
        jax.ShapeDtypeStruct((ts, inner), BF16),
        jax.ShapeDtypeStruct((rows, inner), BF16),
        jax.ShapeDtypeStruct((piece, inner), F32),
        jax.ShapeDtypeStruct((1, per), F32),
    )
    outs = pl.pallas_call(
        functools.partial(joint_kernel, n_dp),
        out_shape=out_shape,
        in_specs=[vmem, vmem, hbm, vmem, vmem, vmem, vmem, hbm, hbm, hbm, hbm, vmem, hbm],
        out_specs=(vmem,) * 5,
        scratch_shapes=[
            pltpu.VMEM(text_proj.shape, BF16),
            pltpu.VMEM(out_weight.shape, BF16),
            pltpu.VMEM((rows, d_model), BF16),
            pltpu.VMEM((NC, NY, NZ, tq, 3 * hg), F32),
            pltpu.VMEM((NY, NZ, tq, 3 * hg), F32),
            *[pltpu.VMEM((n, tq, width), dtype) for n in (NZ, NZ, NZ, 3) for width, dtype in ((hg, F32), (2 * hg, BF16))],
            pltpu.VMEM((8, slots), F32),
            pltpu.VMEM((n_seq - 1, 8, slots), F32),
            pltpu.VMEM((slots, slots), F32),
            pltpu.VMEM((slots, slots), F32),
            pltpu.VMEM((NZ, rows, hg), BF16),
            pltpu.VMEM((tq, hg), BF16),
            pltpu.VMEM((NZ, hg // 128, rows, 128), F32),
            pltpu.VMEM((NZ, hg // 128, rows, 128), F32),
            pltpu.VMEM((NZ, rows, hg), F32),
            pltpu.VMEM((2, n_seq * rows + slots, hg), BF16),
            pltpu.VMEM((rows, d_model), BF16),
            pltpu.VMEM((d_model, rows), F32),
            pltpu.VMEM((NQ, n_dp, blk, rows), BF16),
            pltpu.VMEM((n_dp, blk, n_seq * rows), BF16),
            pltpu.VMEM((n_seq * rows, hg), BF16),
            pltpu.VMEM((NZ, rows, hg), BF16),
            pltpu.VMEM((NZ, ts, hg), F32),
            pltpu.VMEM((NZ, ts, hg), F32),
            pltpu.VMEM((n_dp, NZ, piece, hg), BF16),
            pltpu.VMEM((n_dp, NZ, piece, hg), BF16),
            pltpu.VMEM((NZ, piece, hg), F32),
            pltpu.VMEM((NZ, piece, hg), F32),
            pltpu.VMEM((n_seq, 8, 256), F32),
            pltpu.VMEM((n_seq - 1, 8, 256), F32),
            *[dma(shape) for shape in sems],
        ],
        compiler_params=pltpu.CompilerParams(
            collective_id=0, has_side_effects=True, vmem_limit_bytes=58 * 1024 * 1024
        ),
        name="joint",
    )(
        caption_states[0],
        caption_gain[None],
        text_proj,
        slot_source,
        caption_len[None],
        query_gain[None],
        key_gain[None],
        image_q[0],
        image_k[0],
        image_v[0],
        out_weight,
        gate,
        d_out[0],
    )
    image_out, text_attn, d_attn, grad_wo, grad_gate = pl.pallas_call(
        copy_out,
        out_shape=out_shape,
        in_specs=[vmem] * 5,
        out_specs=(hbm,) * 5,
        scratch_shapes=[dma((5,))],
        name="copy_out",
    )(*outs)
    return (image_out[None], text_attn[None], d_attn[None], grad_wo, grad_gate)


def solution(mesh):
    in_specs = (
        P("dp", None, "seq"),
        P("seq"),
        P("seq", None),
        P("dp"),
        P("dp", None),
        P(),
        P(),
        P("dp", "seq", None),
        P("dp", "seq", None),
        P("dp", "seq", None),
        P(),
        P("dp", None),
        P("dp", "seq", None),
    )
    out_specs = (
        P("dp", "seq", None),
        P("dp", "seq", None),
        P("dp", "seq", None),
        P(("dp", "seq"), None),
        P("dp", "seq"),
    )
    return jax.shard_map(
        functools.partial(on_device, mesh.shape["dp"]),
        mesh=mesh,
        in_specs=in_specs,
        out_specs=out_specs,
        check_vma=False,
    )
```

```python
import functools
import math

import jax
import jax.numpy as jnp
from jax import lax
from jax.experimental import pallas as pl
from jax.experimental.pallas import tpu as pltpu
from jax.sharding import PartitionSpec as P

EPS = 1e-06
NEG_BIG = -1e30
NY, NZ, NC = 2, 4, 2
NQ = NY * NC
F32 = jnp.float32
BF16 = jnp.bfloat16
NT = (((1,), (1,)), ((), ()))


def joint_kernel(
    n_dp,
    states_ref,
    gain_ref,
    text_proj_hbm,
    source_ref,
    length_ref,
    qgain_ref,
    kgain_ref,
    q_hbm,
    k_hbm,
    v_hbm,
    wo_hbm,
    gate_ref,
    dout_hbm,
    image_out_ref,
    text_attn_ref,
    d_attn_ref,
    grad_wo_ref,
    grad_gate_ref,
    tp,
    wo,
    dout,
    part,
    core_recv,
    ysend_q,
    ysend_kv,
    yrecv_q,
    yrecv_kv,
    zsend_q,
    zsend_kv,
    zrecv_q,
    zrecv_kv,
    sq_send,
    sq_recv,
    sq_col,
    src_col,
    qi,
    qt,
    near_top,
    near_sum,
    near_acc,
    kv,
    g,
    gtf,
    gt,
    gt_all,
    a_all,
    a_rows,
    tsend,
    trecv,
    psend,
    precv,
    own_grad,
    fin,
    gsend,
    grecv,
    image_buf,
    d_attn_buf,
    store_sem,
    load_sem,
    loc_sem,
    kvq_s,
    kvq_r,
    fwd_s,
    fwd_r,
    core_s,
    core_r,
    ytx_s,
    ytx_r,
    ztx_s,
    ztx_r,
    sq_s,
    sq_r,
    txkv_s,
    txkv_r,
    g1_s,
    g1_r,
    gz_s,
    gz_r,
    aret_s,
    aret_r,
    tret_s,
    tret_r,
    apl_s,
    apl_r,
    dp_s,
    dp_r,
    gg_s,
    gg_r,
):
    dp = lax.axis_index("dp")
    me = lax.axis_index("seq")
    n_seq = NY * NZ * NC
    y = me // (NZ * NC)
    z = (me // NC) % NZ
    c = me % NC
    q = y * NC + c
    rows, inner = a_rows.shape[1], NZ * a_rows.shape[2]
    hg = a_rows.shape[2]
    head = 128
    n_heads = hg // head
    d_model = dout.shape[1]
    slots = source_ref.shape[1]
    tq = slots // NQ
    ts = tq // NZ
    image_keys = n_seq * rows
    blk = gt.shape[2]
    piece = blk // NZ

    def at_z(z_to):
        return y * (NZ * NC) + z_to * NC + c

    s_y = (1 - y) * (NZ * NC) + z * NC + c
    s_c = y * (NZ * NC) + z * NC + (1 - c)
    s_d = (1 - y) * (NZ * NC) + z * NC + (1 - c)
    q_y = (1 - y) * NC + c
    q_c = y * NC + (1 - c)
    q_d = (1 - y) * NC + (1 - c)

    def to_seq(src, dst, ss, rs, target):
        return pltpu.make_async_remote_copy(
            src_ref=src,
            dst_ref=dst,
            send_sem=ss,
            recv_sem=rs,
            device_id={"seq": target},
            device_id_type=pl.DeviceIdType.MESH,
        )

    def col(index):
        return pl.ds(pl.multiple_of(index * hg, 128), hg)

    def kv_rows(q_from, z_from):
        return pl.ds(pl.multiple_of((q_from * NZ + z_from) * rows, 128), rows)

    barrier = pltpu.get_barrier_semaphore()

    @pl.loop(1, n_seq)
    def _(offset):
        pl.semaphore_signal(
            barrier,
            inc=1,
            device_id={"seq": (me + offset) % n_seq},
            device_id_type=pl.DeviceIdType.MESH,
        )

    @pl.loop(1, n_dp)
    def _(offset):
        for z_to in range(NZ):
            pl.semaphore_signal(
                barrier,
                inc=1,
                device_id={"dp": (dp + offset) % n_dp, "seq": at_z(z_to)},
                device_id_type=pl.DeviceIdType.MESH,
            )

    own_rows = kv_rows(q, z)
    own = [
        pltpu.make_async_copy(k_hbm.at[:, col(z)], kv.at[0, own_rows, :], loc_sem.at[0]),
        pltpu.make_async_copy(v_hbm.at[:, col(z)], kv.at[1, own_rows, :], loc_sem.at[1]),
        pltpu.make_async_copy(q_hbm.at[:, col(z)], qi.at[z], loc_sem.at[2]),
    ]
    for copy in own:
        copy.start()

    load_tp = pltpu.make_async_copy(text_proj_hbm, tp, load_sem.at[0])
    load_dout = pltpu.make_async_copy(dout_hbm, dout, load_sem.at[1])
    load_wo = pltpu.make_async_copy(wo_hbm, wo, load_sem.at[2])
    load_tp.start()
    load_dout.start()
    load_wo.start()

    pl.semaphore_wait(barrier, n_seq - 1 + NZ * (n_dp - 1))

    kvq = {}
    for dz in (2, 1, 3):
        z_to = (z + dz) % NZ
        target = at_z(z_to)
        kvq[dz] = (
            to_seq(k_hbm.at[:, col(z_to)], kv.at[0, own_rows, :], kvq_s.at[0, dz - 1], kvq_r.at[0, dz - 1], target),
            to_seq(v_hbm.at[:, col(z_to)], kv.at[1, own_rows, :], kvq_s.at[1, dz - 1], kvq_r.at[1, dz - 1], target),
            to_seq(q_hbm.at[:, col(z_to)], qi.at[z], kvq_s.at[2, dz - 1], kvq_r.at[2, dz - 1], target),
        )
        kvq[dz][0].start()
        kvq[dz][1].start()
    for dz in (2, 1, 3):
        kvq[dz][2].start()

    def forward(dz):
        block = kv.at[:, kv_rows(q, (z - dz + NZ) % NZ), :]
        return (
            to_seq(block, block, fwd_s.at[0, dz], fwd_r.at[0, dz], s_y),
            to_seq(block, block, fwd_s.at[1, dz], fwd_r.at[1, dz], s_c),
        )

    def relay(dz):
        block = kv.at[:, kv_rows(q_y, (z - dz + NZ) % NZ), :]
        return to_seq(block, block, fwd_s.at[2, dz], fwd_r.at[2, dz], s_c)

    own[0].wait()
    own[1].wait()
    for copy in forward(0):
        copy.start()

    place = lax.broadcasted_iota(jnp.int32, (slots, slots), 0)
    lane = lax.broadcasted_iota(jnp.int32, (slots, slots), 1)
    at_c, at_y = place // (slots // NC), (place // tq) % NY
    slot_of = at_y * (slots // NY) + ((place // ts) % NZ) * (NC * ts) + at_c * ts + place % ts
    order = jnp.where(lane == slot_of, 1.0, 0.0).astype(BF16)
    row_at_slot = jnp.where(place == source_ref[...], 1.0, 0.0).astype(BF16)
    onehot = lax.dot_general(order, row_at_slot, NT, preferred_element_type=F32)
    src_col[...] = jnp.broadcast_to(
        jnp.sum(onehot * lane.astype(F32), axis=1, keepdims=True), (slots, slots)
    )
    onehot = onehot.astype(BF16)
    src_row = lax.dot_general(lane[:8].astype(F32).astype(BF16), onehot, NT, preferred_element_type=F32)
    picked = jnp.dot(onehot, states_ref[...], preferred_element_type=F32)
    scaled = (picked * gain_ref[...]).astype(BF16)
    squares = jnp.sum(picked * picked, axis=1, keepdims=True)
    sq_send[...] = jnp.transpose(jnp.broadcast_to(squares, (slots, slots)))[:8]

    load_tp.wait()
    for zz in range(NZ):
        for kind in range(3):
            block = jnp.dot(
                scaled,
                tp[:, kind * inner + zz * hg : kind * inner + (zz + 1) * hg],
                preferred_element_type=F32,
            )
            for i in range(NQ):
                part[i // NY, i % NY, zz, :, kind * hg : (kind + 1) * hg] = block[i * tq : (i + 1) * tq]

    core_copy = to_seq(part.at[1 - c], core_recv, core_s.at[0], core_r.at[0], s_c)
    core_copy.start()

    def square_copy(offset):
        target = (me + offset) % n_seq
        return to_seq(sq_send, sq_recv.at[offset - 1], sq_s.at[offset - 1], sq_r.at[offset - 1], target)

    @pl.loop(1, n_seq)
    def _(offset):
        square_copy(offset).start()

    load_dout.wait()
    for t in range(d_model // 128):
        cols = slice(t * 128, (t + 1) * 128)
        gated = gate_ref[:, cols] * dout[:, cols].astype(F32)
        g[:, cols] = gated.astype(BF16)
        gtf[cols, :] = jnp.transpose(gated)

    core_copy.wait_recv()
    for zz in range(NZ):
        summed = part[c, 1 - y, zz] + core_recv[1 - y, zz]
        ysend_q[zz] = summed[:, :hg]
        ysend_kv[zz] = summed[:, hg:].astype(BF16)
    y_copies = (
        to_seq(ysend_q, yrecv_q, ytx_s.at[0], ytx_r.at[0], s_y),
        to_seq(ysend_kv, yrecv_kv, ytx_s.at[1], ytx_r.at[1], s_y),
    )
    for copy in y_copies:
        copy.start()

    for p in range(n_dp):
        for qq in range(NQ):
            pieces = []
            for zz in range(NZ):
                owner = (qq // NC) * (NZ * NC) + zz * NC + qq % NC
                start = (p * n_seq + owner) * piece
                pieces.append(gtf[start : start + piece, :])
            gt[qq, p] = jnp.concatenate(pieces, axis=0).astype(BF16)

    def gcols(q_from, z_from):
        return pl.ds(pl.multiple_of((q_from * NZ + z_from) * rows, 128), rows)

    g1 = [
        to_seq(gt.at[q_to], gt_all.at[:, :, gcols(q, z)], g1_s.at[i], g1_r.at[i], target)
        for i, (q_to, target) in enumerate(((q_y, s_y), (q_c, s_c), (q_d, s_d)))
    ]
    g1[1].start()
    own_g = pltpu.make_async_copy(gt.at[q], gt_all.at[:, :, gcols(q, z)], loc_sem.at[3])
    own_g.start()

    ahead = 1 - 2 * c
    z_p = (z + ahead + NZ) % NZ
    z_n = (z - ahead + NZ) % NZ

    def g_ahead(i, q_from):
        block = gt_all.at[:, :, gcols(q_from, z)]
        return (
            to_seq(block, block, gz_s.at[0, i], gz_r.at[0, i], at_z(z_p)),
            to_seq(block, block, gz_s.at[1, i], gz_r.at[1, i], at_z(z_n)),
        )

    def g_relay(i, q_from):
        block = gt_all.at[:, :, gcols(q_from, z_n)]
        return to_seq(block, block, gz_s.at[2, i], gz_r.at[2, i], at_z(z_p))

    load_wo.wait()
    for t in range(inner // 256):
        cols = slice(t * 256, (t + 1) * 256)
        d_attn_buf[:, cols] = jnp.dot(g[...], wo[:, cols], preferred_element_type=F32).astype(BF16)
    store_d_attn = pltpu.make_async_copy(d_attn_buf, d_attn_ref, store_sem.at[0])
    store_d_attn.start()

    for dz in (1, 3, 2):
        kvq[dz][0].wait_recv()
        kvq[dz][1].wait_recv()
        for copy in forward(dz):
            copy.start()

    g1[0].start()
    g1[2].start()

    for copy in y_copies:
        copy.wait_recv()
    for zz in range(NZ):
        summed = part[c, y, zz] + core_recv[y, zz]
        zsend_q[zz] = summed[:, :hg] + yrecv_q[zz]
        part[c, y, zz, :, hg:] = summed[:, hg:] + yrecv_kv[zz].astype(F32)
        zsend_kv[zz] = part[c, y, zz, :, hg:].astype(BF16)

    z_copies = []
    for dz in (2, 1, 3):
        z_to = (z + dz) % NZ
        for kind, (src, dst) in enumerate(((zsend_q, zrecv_q), (zsend_kv, zrecv_kv))):
            copy = to_seq(
                src.at[z_to], dst.at[dz - 1], ztx_s.at[kind, dz - 1], ztx_r.at[kind, dz - 1], at_z(z_to)
            )
            copy.start()
            z_copies.append(copy)

    own_g.wait()
    for copy in g_ahead(0, q):
        copy.start()
    g1[1].wait_recv()
    for copy in g_ahead(2, q_c):
        copy.start()

    own[2].wait()
    for dz in (1, 3, 2):
        kvq[dz][2].wait_recv()
    for dz in (0, 1, 3, 2):
        forward(dz)[1].wait_recv()

    factor = head ** (-0.5) * math.log2(math.e)
    half = image_keys // NY
    near_rows = pl.ds(pl.multiple_of(y * half, 128), half)
    far_rows = pl.ds(pl.multiple_of((1 - y) * half, 128), half)

    def attend_near(query, h):
        cols = slice(h * head, (h + 1) * head)
        scores = lax.dot_general(query, kv[0, near_rows, cols], NT, preferred_element_type=F32)
        top = jnp.max(scores, axis=1, keepdims=True)
        probs = jnp.exp2((scores - top) * factor)
        values = jnp.dot(probs.astype(BF16), kv[1, near_rows, cols], preferred_element_type=F32)
        return top, jnp.sum(probs, axis=1, keepdims=True), values

    for i in range(NZ):
        z_to = (z + i + 1) % NZ
        for h in range(n_heads):
            cols = slice(h * head, (h + 1) * head)
            top, total, values = attend_near(qi[z_to, :, cols], h)
            near_top[i, h] = jnp.broadcast_to(top, (rows, head))
            near_sum[i, h] = jnp.broadcast_to(total, (rows, head))
            near_acc[i, :, cols] = values
        dz = (0, 1, 3, 2)[i]
        forward(dz)[0].wait_recv()
        relay(dz).start()

    def add_square(offset, total):
        square_copy(offset).wait_recv()
        return total + sq_recv[offset - 1]

    square_row = lax.fori_loop(1, n_seq, add_square, sq_send[...])
    sq_col[...] = jnp.transpose(jnp.broadcast_to(square_row[0:1], (slots, slots)))
    own_slots = pl.ds(pl.multiple_of((c * NY + y) * tq, 32), tq)
    rate = lax.rsqrt(sq_col[own_slots, 0:1] / (n_seq * states_ref.shape[1]) + EPS)
    for copy in z_copies:
        copy.wait_recv()
    total_q = zsend_q[z]
    total_kv = part[c, y, z, :, hg:]
    for dz in range(1, NZ):
        total_q += zrecv_q[dz - 1]
        total_kv += zrecv_kv[dz - 1].astype(F32)
    normed_q, normed_kv = total_q * rate, total_kv * rate
    text_rows = pl.ds(pl.multiple_of(image_keys + (c * NY + y) * tq, 32), tq)
    for h in range(n_heads):
        cols = slice(h * head, (h + 1) * head)
        x = normed_q[:, cols]
        qt[:, cols] = (x * lax.rsqrt(jnp.mean(x * x, axis=1, keepdims=True) + EPS) * qgain_ref[...]).astype(BF16)
        x = normed_kv[:, cols]
        kv[0, text_rows, cols] = (
            x * lax.rsqrt(jnp.mean(x * x, axis=1, keepdims=True) + EPS) * kgain_ref[...]
        ).astype(BF16)
    kv[1, text_rows, :] = normed_kv[:, hg:].astype(BF16)
    text_block = kv.at[:, text_rows, :]
    txkv = []
    for i, target in enumerate((s_y, s_c, s_d)):
        copy = to_seq(text_block, text_block, txkv_s.at[i], txkv_r.at[i], target)
        copy.start()
        txkv.append(copy)

    for i, q_from in ((1, q_y), (3, q_d)):
        g1[i - 1].wait_recv()
        for copy in g_ahead(i, q_from):
            copy.start()
    for dz in (0, 1, 3, 2):
        relay(dz).wait_recv()
    for copy in txkv:
        copy.wait_recv()

    length = length_ref[...].astype(F32)
    bias = jnp.where(src_row[0:1] < length, 0.0, NEG_BIG)

    def attend(query, h, near):
        cols = slice(h * head, (h + 1) * head)
        near_max, near_total, near_values = near
        image_scores = lax.dot_general(query, kv[0, far_rows, cols], NT, preferred_element_type=F32)
        text_scores = lax.dot_general(query, kv[0, image_keys:, cols], NT, preferred_element_type=F32) + bias
        top = jnp.maximum(
            jnp.max(image_scores, axis=1, keepdims=True), jnp.max(text_scores, axis=1, keepdims=True)
        )
        top = jnp.maximum(top, near_max)
        image_probs = jnp.exp2((image_scores - top) * factor)
        text_probs = jnp.exp2((text_scores - top) * factor)
        scale = jnp.exp2((near_max - top) * factor)
        denom = jnp.sum(image_probs, axis=1, keepdims=True) + jnp.sum(text_probs, axis=1, keepdims=True)
        summed = jnp.dot(image_probs.astype(BF16), kv[1, far_rows, cols], preferred_element_type=F32)
        summed += jnp.dot(text_probs.astype(BF16), kv[1, image_keys:, cols], preferred_element_type=F32)
        return (summed + scale * near_values) / (denom + scale * near_total)

    def a_block(q_from, z_of):
        return a_all.at[kv_rows(q_from, z_of), :]

    def a_return(i):
        z_to = (z + i + 1) % NZ
        return to_seq(a_block(q, z_to), a_rows.at[z], aret_s.at[i], aret_r.at[i], at_z(z_to))

    def a_plane(i):
        block = a_block(q, (z + i + 1) % NZ)
        return (
            to_seq(block, block, apl_s.at[0, i], apl_r.at[0, i], s_y),
            to_seq(block, block, apl_s.at[1, i], apl_r.at[1, i], s_c),
        )

    def a_relay(i):
        block = a_block(q_y, (z + i + 1) % NZ)
        return to_seq(block, block, apl_s.at[2, i], apl_r.at[2, i], s_c)

    def g_source(i):
        y_from = (y + i % 2) % NY
        c_from = (c + i // 2) % NC
        return y_from * NC + c_from

    @pl.loop(0, NZ)
    def _(i):
        z_to = (z + i + 1) % NZ
        for h in range(n_heads):
            cols = slice(h * head, (h + 1) * head)
            near = near_top[i, h][:, :1], near_sum[i, h][:, :1], near_acc[i, :, cols]
            result = attend(qi[z_to, :, cols], h, near)
            a_all[kv_rows(q, z_to), cols] = result.astype(BF16)

        @pl.when(i < NZ - 1)
        def _():
            a_return(i).start()

        for copy in a_plane(i):
            copy.start()
        k = (i % 2) * 2 + i // 2
        source = g_source(k)
        g_ahead(k, source)[0].wait_recv()
        g_relay(k, source).start()

        @pl.when(i > 0)
        def _():
            a_plane(i - 1)[0].wait_recv()
            a_relay(i - 1).start()

    a_rows[z] = a_all[kv_rows(q, z), :]

    slot_valid = src_col[own_slots, 0:1] < length
    for h in range(n_heads):
        cols = slice(h * head, (h + 1) * head)
        result = jnp.where(slot_valid, attend(qt[:, cols], h, attend_near(qt[:, cols], h)), 0.0)
        for zz in range(NZ):
            tsend[zz, :, cols] = result[zz * ts : (zz + 1) * ts, :]

    def t_return(dz):
        z_to = (z + dz) % NZ
        return to_seq(tsend.at[z_to], trecv.at[z], tret_s.at[dz - 1], tret_r.at[dz - 1], at_z(z_to))

    for dz in range(1, NZ):
        t_return(dz).start()
    trecv[z] = tsend[z]

    a_plane(NZ - 1)[0].wait_recv()
    a_relay(NZ - 1).start()

    for i in range(NZ - 1):
        a_return(i).wait_recv()
    image_attn = jnp.concatenate([a_rows[zz] for zz in range(NZ)], axis=1)
    per = d_model // n_seq
    for t in range(n_seq // 2):
        cols = slice(t * 2 * per, (t + 1) * 2 * per)
        projected = lax.dot_general(image_attn, wo[cols, :], NT, preferred_element_type=F32)
        image_buf[:, cols] = (gate_ref[:, cols] * projected).astype(BF16)
        term = jnp.sum(projected * dout[:, cols].astype(F32), axis=0, keepdims=True)
        gsend[2 * t, :, :per] = jnp.broadcast_to(term[:, :per], (8, per))
        gsend[2 * t + 1, :, :per] = jnp.broadcast_to(term[:, per:], (8, per))

    store_image = pltpu.make_async_copy(image_buf, image_out_ref, store_sem.at[1])
    store_image.start()

    def gate_copy(offset):
        target = (me + offset) % n_seq
        return to_seq(gsend.at[target], grecv.at[offset - 1], gg_s.at[offset - 1], gg_r.at[offset - 1], target)

    @pl.loop(1, n_seq)
    def _(offset):
        gate_copy(offset).start()

    @pl.loop(0, NZ)
    def _(i):
        source = g_source(i)
        g_ahead(i, source)[1].wait_recv()
        g_relay(i, source).wait_recv()
        a_plane(i)[1].wait_recv()
        a_relay(i).wait_recv()

    def grad_block(p):
        return jnp.dot(gt_all[p], a_all[...], preferred_element_type=F32)

    def dp_copy(jd, jz):
        p, z_to = (dp + jd) % n_dp, (z + jz) % NZ
        return pltpu.make_async_remote_copy(
            src_ref=psend.at[p, z_to],
            dst_ref=precv.at[jd, jz],
            send_sem=dp_s.at[jd, jz],
            recv_sem=dp_r.at[jd, jz],
            device_id={"dp": p, "seq": at_z(z_to)},
            device_id_type=pl.DeviceIdType.MESH,
        )

    @pl.loop(1, n_dp)
    def _(jd):
        p = (dp + jd) % n_dp
        block = grad_block(p)
        for zz in range(NZ):
            psend[p, zz] = block[zz * piece : (zz + 1) * piece].astype(BF16)
        for jz in range(NZ):
            dp_copy(jd, jz).start()

    block = grad_block(dp)
    for zz in range(NZ):
        own_grad[zz] = block[zz * piece : (zz + 1) * piece]
        psend[dp, zz] = block[zz * piece : (zz + 1) * piece].astype(BF16)
    for jz in range(1, NZ):
        dp_copy(0, jz).start()

    for dz in range(1, NZ):
        t_return(dz).wait_recv()
    for zz in range(NZ):
        text_attn_ref[:, zz * hg : (zz + 1) * hg] = trecv[zz].astype(BF16)

    def add_gate(offset, total):
        gate_copy(offset).wait_recv()
        return total + grecv[offset - 1]

    gate_total = lax.fori_loop(1, n_seq, add_gate, gsend[me])
    grad_gate_ref[...] = gate_total[0:1, :per]

    for jz in range(NZ):
        if jz:
            dp_copy(0, jz).wait_recv()
            first = precv[0, jz].astype(F32)
        else:
            first = own_grad[z]

        def add_grad(jd, total):
            dp_copy(jd, jz).wait_recv()
            return total + precv[jd, jz].astype(F32)

        fin[(z - jz + NZ) % NZ] = lax.fori_loop(1, n_dp, add_grad, first)
    for zz in range(NZ):
        grad_wo_ref[:, zz * hg : (zz + 1) * hg] = fin[zz]

    store_d_attn.wait()
    store_image.wait()
    for dz in range(1, NZ):
        for copy in kvq[dz]:
            copy.wait_send()
        t_return(dz).wait_send()
        a_return(dz - 1).wait_send()
        dp_copy(0, dz).wait_send()
    for copy in (*g1, *txkv, *y_copies, *z_copies, core_copy):
        copy.wait_send()

    @pl.loop(0, NZ)
    def _(i):
        source = g_source(i)
        for copy in (*forward(i), relay(i), *g_ahead(i, source), g_relay(i, source), *a_plane(i), a_relay(i)):
            copy.wait_send()

    @pl.loop(1, n_seq)
    def _(offset):
        square_copy(offset).wait_send()
        gate_copy(offset).wait_send()

    @pl.loop(1, n_dp)
    def _(jd):
        for jz in range(NZ):
            dp_copy(jd, jz).wait_send()


def copy_out(*refs):
    sources, results, sem = refs[:5], refs[5:10], refs[10]
    copies = [
        pltpu.make_async_copy(src, dst, sem.at[i]) for i, (src, dst) in enumerate(zip(sources, results))
    ]
    for copy in copies:
        copy.start()
    for copy in copies:
        copy.wait()


def on_device(
    n_dp,
    caption_states,
    caption_gain,
    text_proj,
    caption_len,
    slot_source,
    query_gain,
    key_gain,
    image_q,
    image_k,
    image_v,
    out_weight,
    gate,
    d_out,
):
    slots = slot_source.shape[1]
    rows, inner = image_q.shape[1:]
    d_model = d_out.shape[2]
    n_seq = NY * NZ * NC
    hg = inner // NZ
    tq = slots // NQ
    ts = tq // NZ
    blk = d_model // n_dp // NQ
    piece = blk // NZ
    per = d_model // n_seq
    vmem = pl.BlockSpec(memory_space=pltpu.VMEM)
    hbm = pl.BlockSpec(memory_space=pl.ANY)
    dma = pltpu.SemaphoreType.DMA
    sems = [
        (3,), (4,), (3, 3), (3, 3), (3, NZ), (3, NZ), (1,), (1,), (2,), (2,), (2, 3), (2, 3), (n_seq - 1,),
        (n_seq - 1,), (3,), (3,), (3,), (3,), (3, NZ), (3, NZ), (3,), (3,), (3,), (3,), (3, NZ), (3, NZ),
        (n_dp, NZ), (n_dp, NZ), (n_seq - 1,), (n_seq - 1,),
    ]
    out_shape = (
        jax.ShapeDtypeStruct((rows, d_model), BF16),
        jax.ShapeDtypeStruct((ts, inner), BF16),
        jax.ShapeDtypeStruct((rows, inner), BF16),
        jax.ShapeDtypeStruct((piece, inner), F32),
        jax.ShapeDtypeStruct((1, per), F32),
    )
    outs = pl.pallas_call(
        functools.partial(joint_kernel, n_dp),
        out_shape=out_shape,
        in_specs=[vmem, vmem, hbm, vmem, vmem, vmem, vmem, hbm, hbm, hbm, hbm, vmem, hbm],
        out_specs=(hbm, vmem, hbm, vmem, vmem),
        scratch_shapes=[
            pltpu.VMEM(text_proj.shape, BF16),
            pltpu.VMEM(out_weight.shape, BF16),
            pltpu.VMEM((rows, d_model), BF16),
            pltpu.VMEM((NC, NY, NZ, tq, 3 * hg), F32),
            pltpu.VMEM((NY, NZ, tq, 3 * hg), F32),
            *[pltpu.VMEM((n, tq, width), dtype) for n in (NZ, NZ, NZ, 3) for width, dtype in ((hg, F32), (2 * hg, BF16))],
            pltpu.VMEM((8, slots), F32),
            pltpu.VMEM((n_seq - 1, 8, slots), F32),
            pltpu.VMEM((slots, slots), F32),
            pltpu.VMEM((slots, slots), F32),
            pltpu.VMEM((NZ, rows, hg), BF16),
            pltpu.VMEM((tq, hg), BF16),
            pltpu.VMEM((NZ, hg // 128, rows, 128), F32),
            pltpu.VMEM((NZ, hg // 128, rows, 128), F32),
            pltpu.VMEM((NZ, rows, hg), F32),
            pltpu.VMEM((2, n_seq * rows + slots, hg), BF16),
            pltpu.VMEM((rows, d_model), BF16),
            pltpu.VMEM((d_model, rows), F32),
            pltpu.VMEM((NQ, n_dp, blk, rows), BF16),
            pltpu.VMEM((n_dp, blk, n_seq * rows), BF16),
            pltpu.VMEM((n_seq * rows, hg), BF16),
            pltpu.VMEM((NZ, rows, hg), BF16),
            pltpu.VMEM((NZ, ts, hg), F32),
            pltpu.VMEM((NZ, ts, hg), F32),
            pltpu.VMEM((n_dp, NZ, piece, hg), BF16),
            pltpu.VMEM((n_dp, NZ, piece, hg), BF16),
            pltpu.VMEM((NZ, piece, hg), F32),
            pltpu.VMEM((NZ, piece, hg), F32),
            pltpu.VMEM((n_seq, 8, 256), F32),
            pltpu.VMEM((n_seq - 1, 8, 256), F32),
            pltpu.VMEM((rows, d_model), BF16),
            pltpu.VMEM((rows, inner), BF16),
            dma((2,)),
            *[dma(shape) for shape in sems],
        ],
        compiler_params=pltpu.CompilerParams(
            collective_id=0, has_side_effects=True, vmem_limit_bytes=58 * 1024 * 1024
        ),
        name="joint",
    )(
        caption_states[0],
        caption_gain[None],
        text_proj,
        slot_source,
        caption_len[None],
        query_gain[None],
        key_gain[None],
        image_q[0],
        image_k[0],
        image_v[0],
        out_weight,
        gate,
        d_out[0],
    )
    image_out, text_attn, d_attn, grad_wo, grad_gate = pl.pallas_call(
        copy_out,
        out_shape=out_shape,
        in_specs=[vmem] * 5,
        out_specs=(hbm,) * 5,
        scratch_shapes=[dma((5,))],
        name="copy_out",
    )(*outs)
    return (image_out[None], text_attn[None], d_attn[None], grad_wo, grad_gate)


def solution(mesh):
    in_specs = (
        P("dp", None, "seq"),
        P("seq"),
        P("seq", None),
        P("dp"),
        P("dp", None),
        P(),
        P(),
        P("dp", "seq", None),
        P("dp", "seq", None),
        P("dp", "seq", None),
        P(),
        P("dp", None),
        P("dp", "seq", None),
    )
    out_specs = (
        P("dp", "seq", None),
        P("dp", "seq", None),
        P("dp", "seq", None),
        P(("dp", "seq"), None),
        P("dp", "seq"),
    )
    return jax.shard_map(
        functools.partial(on_device, mesh.shape["dp"]),
        mesh=mesh,
        in_specs=in_specs,
        out_specs=out_specs,
        check_vma=False,
    )
```

```python
import functools
import math

import jax
import jax.numpy as jnp
from jax import lax
from jax.experimental import pallas as pl
from jax.experimental.pallas import tpu as pltpu
from jax.sharding import PartitionSpec as P

EPS = 1e-06
NEG_BIG = -1e30
NY, NZ, NC = 2, 4, 2
NQ = NY * NC
F32 = jnp.float32
BF16 = jnp.bfloat16
NT = (((1,), (1,)), ((), ()))


def joint_kernel(
    n_dp,
    states_ref,
    gain_ref,
    text_proj_hbm,
    source_ref,
    length_ref,
    qgain_ref,
    kgain_ref,
    q_hbm,
    k_hbm,
    v_hbm,
    wo_hbm,
    gate_ref,
    dout_hbm,
    image_out_ref,
    text_attn_ref,
    d_attn_ref,
    grad_wo_ref,
    grad_gate_ref,
    tp,
    wo,
    dout,
    part,
    core_recv,
    ysend_q,
    ysend_kv,
    yrecv_q,
    yrecv_kv,
    zsend_q,
    zsend_kv,
    zrecv_q,
    zrecv_kv,
    sq_send,
    sq_recv,
    sq_col,
    src_col,
    qi,
    qt,
    near_top,
    near_sum,
    near_acc,
    kv,
    g,
    gtf,
    gt,
    gt_all,
    a_all,
    a_rows,
    tsend,
    trecv,
    psend,
    precv,
    own_grad,
    fin,
    gsend,
    grecv,
    image_buf,
    d_attn_buf,
    store_sem,
    load_sem,
    loc_sem,
    kvq_s,
    kvq_r,
    fwd_s,
    fwd_r,
    core_s,
    core_r,
    ytx_s,
    ytx_r,
    ztx_s,
    ztx_r,
    sq_s,
    sq_r,
    txkv_s,
    txkv_r,
    g1_s,
    g1_r,
    gz_s,
    gz_r,
    aret_s,
    aret_r,
    tret_s,
    tret_r,
    apl_s,
    apl_r,
    dp_s,
    dp_r,
    gg_s,
    gg_r,
):
    dp = lax.axis_index("dp")
    me = lax.axis_index("seq")
    n_seq = NY * NZ * NC
    y = me // (NZ * NC)
    z = (me // NC) % NZ
    c = me % NC
    q = y * NC + c
    rows, inner = a_rows.shape[1], NZ * a_rows.shape[2]
    hg = a_rows.shape[2]
    head = 128
    n_heads = hg // head
    d_model = dout.shape[1]
    slots = source_ref.shape[1]
    tq = slots // NQ
    ts = tq // NZ
    image_keys = n_seq * rows
    blk = gt.shape[2]
    piece = blk // NZ

    def at_z(z_to):
        return y * (NZ * NC) + z_to * NC + c

    s_y = (1 - y) * (NZ * NC) + z * NC + c
    s_c = y * (NZ * NC) + z * NC + (1 - c)
    s_d = (1 - y) * (NZ * NC) + z * NC + (1 - c)
    q_y = (1 - y) * NC + c
    q_c = y * NC + (1 - c)
    q_d = (1 - y) * NC + (1 - c)

    def to_seq(src, dst, ss, rs, target):
        return pltpu.make_async_remote_copy(
            src_ref=src,
            dst_ref=dst,
            send_sem=ss,
            recv_sem=rs,
            device_id={"seq": target},
            device_id_type=pl.DeviceIdType.MESH,
        )

    def col(index):
        return pl.ds(pl.multiple_of(index * hg, 128), hg)

    def kv_rows(q_from, z_from):
        return pl.ds(pl.multiple_of((q_from * NZ + z_from) * rows, 128), rows)

    barrier = pltpu.get_barrier_semaphore()

    @pl.loop(1, n_seq)
    def _(offset):
        pl.semaphore_signal(
            barrier,
            inc=1,
            device_id={"seq": (me + offset) % n_seq},
            device_id_type=pl.DeviceIdType.MESH,
        )

    @pl.loop(1, n_dp)
    def _(offset):
        for z_to in range(NZ):
            pl.semaphore_signal(
                barrier,
                inc=1,
                device_id={"dp": (dp + offset) % n_dp, "seq": at_z(z_to)},
                device_id_type=pl.DeviceIdType.MESH,
            )

    own_rows = kv_rows(q, z)
    own = [
        pltpu.make_async_copy(k_hbm.at[:, col(z)], kv.at[0, own_rows, :], loc_sem.at[0]),
        pltpu.make_async_copy(v_hbm.at[:, col(z)], kv.at[1, own_rows, :], loc_sem.at[1]),
        pltpu.make_async_copy(q_hbm.at[:, col(z)], qi.at[z], loc_sem.at[2]),
    ]
    for copy in own:
        copy.start()

    load_tp = pltpu.make_async_copy(text_proj_hbm, tp, load_sem.at[0])
    load_dout = pltpu.make_async_copy(dout_hbm, dout, load_sem.at[1])
    load_wo = pltpu.make_async_copy(wo_hbm, wo, load_sem.at[2])
    load_tp.start()
    load_dout.start()
    load_wo.start()

    pl.semaphore_wait(barrier, n_seq - 1 + NZ * (n_dp - 1))

    kvq = {}
    for dz in (2, 1, 3):
        z_to = (z + dz) % NZ
        target = at_z(z_to)
        kvq[dz] = (
            to_seq(k_hbm.at[:, col(z_to)], kv.at[0, own_rows, :], kvq_s.at[0, dz - 1], kvq_r.at[0, dz - 1], target),
            to_seq(v_hbm.at[:, col(z_to)], kv.at[1, own_rows, :], kvq_s.at[1, dz - 1], kvq_r.at[1, dz - 1], target),
            to_seq(q_hbm.at[:, col(z_to)], qi.at[z], kvq_s.at[2, dz - 1], kvq_r.at[2, dz - 1], target),
        )
        kvq[dz][0].start()
        kvq[dz][1].start()
    for dz in (2, 1, 3):
        kvq[dz][2].start()

    def forward(dz):
        block = kv.at[:, kv_rows(q, (z - dz + NZ) % NZ), :]
        return (
            to_seq(block, block, fwd_s.at[0, dz], fwd_r.at[0, dz], s_y),
            to_seq(block, block, fwd_s.at[1, dz], fwd_r.at[1, dz], s_c),
        )

    def relay(dz):
        block = kv.at[:, kv_rows(q_y, (z - dz + NZ) % NZ), :]
        return to_seq(block, block, fwd_s.at[2, dz], fwd_r.at[2, dz], s_c)

    own[0].wait()
    own[1].wait()
    for copy in forward(0):
        copy.start()

    place = lax.broadcasted_iota(jnp.int32, (slots, slots), 0)
    lane = lax.broadcasted_iota(jnp.int32, (slots, slots), 1)
    at_c, at_y = place // (slots // NC), (place // tq) % NY
    slot_of = at_y * (slots // NY) + ((place // ts) % NZ) * (NC * ts) + at_c * ts + place % ts
    order = jnp.where(lane == slot_of, 1.0, 0.0).astype(BF16)
    row_at_slot = jnp.where(place == source_ref[...], 1.0, 0.0).astype(BF16)
    onehot = lax.dot_general(order, row_at_slot, NT, preferred_element_type=F32)
    src_col[...] = jnp.broadcast_to(
        jnp.sum(onehot * lane.astype(F32), axis=1, keepdims=True), (slots, slots)
    )
    onehot = onehot.astype(BF16)
    src_row = lax.dot_general(lane[:8].astype(F32).astype(BF16), onehot, NT, preferred_element_type=F32)
    picked = jnp.dot(onehot, states_ref[...], preferred_element_type=F32)
    scaled = (picked * gain_ref[...]).astype(BF16)
    squares = jnp.sum(picked * picked, axis=1, keepdims=True)
    sq_send[...] = jnp.transpose(jnp.broadcast_to(squares, (slots, slots)))[:8]

    load_tp.wait()
    for zz in range(NZ):
        for kind in range(3):
            block = jnp.dot(
                scaled,
                tp[:, kind * inner + zz * hg : kind * inner + (zz + 1) * hg],
                preferred_element_type=F32,
            )
            for i in range(NQ):
                part[i // NY, i % NY, zz, :, kind * hg : (kind + 1) * hg] = block[i * tq : (i + 1) * tq]

    core_copy = to_seq(part.at[1 - c], core_recv, core_s.at[0], core_r.at[0], s_c)
    core_copy.start()

    def square_copy(offset):
        target = (me + offset) % n_seq
        return to_seq(sq_send, sq_recv.at[offset - 1], sq_s.at[offset - 1], sq_r.at[offset - 1], target)

    @pl.loop(1, n_seq)
    def _(offset):
        square_copy(offset).start()

    load_dout.wait()
    for t in range(d_model // 128):
        cols = slice(t * 128, (t + 1) * 128)
        gated = gate_ref[:, cols] * dout[:, cols].astype(F32)
        g[:, cols] = gated.astype(BF16)
        gtf[cols, :] = jnp.transpose(gated)

    core_copy.wait_recv()
    for zz in range(NZ):
        summed = part[c, 1 - y, zz] + core_recv[1 - y, zz]
        ysend_q[zz] = summed[:, :hg]
        ysend_kv[zz] = summed[:, hg:].astype(BF16)
    y_copies = (
        to_seq(ysend_q, yrecv_q, ytx_s.at[0], ytx_r.at[0], s_y),
        to_seq(ysend_kv, yrecv_kv, ytx_s.at[1], ytx_r.at[1], s_y),
    )
    for copy in y_copies:
        copy.start()

    for p in range(n_dp):
        for qq in range(NQ):
            pieces = []
            for zz in range(NZ):
                owner = (qq // NC) * (NZ * NC) + zz * NC + qq % NC
                start = (p * n_seq + owner) * piece
                pieces.append(gtf[start : start + piece, :])
            gt[qq, p] = jnp.concatenate(pieces, axis=0).astype(BF16)

    def gcols(q_from, z_from):
        return pl.ds(pl.multiple_of((q_from * NZ + z_from) * rows, 128), rows)

    g1 = [
        to_seq(gt.at[q_to], gt_all.at[:, :, gcols(q, z)], g1_s.at[i], g1_r.at[i], target)
        for i, (q_to, target) in enumerate(((q_y, s_y), (q_c, s_c), (q_d, s_d)))
    ]
    g1[1].start()
    own_g = pltpu.make_async_copy(gt.at[q], gt_all.at[:, :, gcols(q, z)], loc_sem.at[3])
    own_g.start()

    ahead = 1 - 2 * c
    z_p = (z + ahead + NZ) % NZ
    z_n = (z - ahead + NZ) % NZ

    def g_ahead(i, q_from):
        block = gt_all.at[:, :, gcols(q_from, z)]
        return (
            to_seq(block, block, gz_s.at[0, i], gz_r.at[0, i], at_z(z_p)),
            to_seq(block, block, gz_s.at[1, i], gz_r.at[1, i], at_z(z_n)),
        )

    def g_relay(i, q_from):
        block = gt_all.at[:, :, gcols(q_from, z_n)]
        return to_seq(block, block, gz_s.at[2, i], gz_r.at[2, i], at_z(z_p))

    load_wo.wait()
    for t in range(inner // 256):
        cols = slice(t * 256, (t + 1) * 256)
        d_attn_buf[:, cols] = jnp.dot(g[...], wo[:, cols], preferred_element_type=F32).astype(BF16)
    store_d_attn = pltpu.make_async_copy(d_attn_buf, d_attn_ref, store_sem.at[0])
    store_d_attn.start()

    for dz in (1, 3, 2):
        kvq[dz][0].wait_recv()
        kvq[dz][1].wait_recv()
        for copy in forward(dz):
            copy.start()

    g1[0].start()
    g1[2].start()

    for copy in y_copies:
        copy.wait_recv()
    for zz in range(NZ):
        summed = part[c, y, zz] + core_recv[y, zz]
        zsend_q[zz] = summed[:, :hg] + yrecv_q[zz]
        part[c, y, zz, :, hg:] = summed[:, hg:] + yrecv_kv[zz].astype(F32)
        zsend_kv[zz] = part[c, y, zz, :, hg:].astype(BF16)

    z_copies = []
    for dz in (2, 1, 3):
        z_to = (z + dz) % NZ
        for kind, (src, dst) in enumerate(((zsend_q, zrecv_q), (zsend_kv, zrecv_kv))):
            copy = to_seq(
                src.at[z_to], dst.at[dz - 1], ztx_s.at[kind, dz - 1], ztx_r.at[kind, dz - 1], at_z(z_to)
            )
            copy.start()
            z_copies.append(copy)

    own_g.wait()
    for copy in g_ahead(0, q):
        copy.start()
    g1[1].wait_recv()
    for copy in g_ahead(2, q_c):
        copy.start()

    own[2].wait()
    for dz in (1, 3, 2):
        kvq[dz][2].wait_recv()
    for dz in (0, 1, 3, 2):
        forward(dz)[1].wait_recv()

    factor = head ** (-0.5) * math.log2(math.e)
    half = image_keys // NY
    near_rows = pl.ds(pl.multiple_of(y * half, 128), half)
    far_rows = pl.ds(pl.multiple_of((1 - y) * half, 128), half)

    def attend_near(query, h):
        cols = slice(h * head, (h + 1) * head)
        scores = lax.dot_general(query, kv[0, near_rows, cols], NT, preferred_element_type=F32)
        top = jnp.max(scores, axis=1, keepdims=True)
        probs = jnp.exp2((scores - top) * factor)
        values = jnp.dot(probs.astype(BF16), kv[1, near_rows, cols], preferred_element_type=F32)
        return top, jnp.sum(probs, axis=1, keepdims=True), values

    for i in range(NZ):
        z_to = (z + i + 1) % NZ
        for h in range(n_heads):
            cols = slice(h * head, (h + 1) * head)
            top, total, values = attend_near(qi[z_to, :, cols], h)
            near_top[i, h] = jnp.broadcast_to(top, (rows, head))
            near_sum[i, h] = jnp.broadcast_to(total, (rows, head))
            near_acc[i, :, cols] = values
        dz = (0, 1, 3, 2)[i]
        forward(dz)[0].wait_recv()
        relay(dz).start()

    def add_square(offset, total):
        square_copy(offset).wait_recv()
        return total + sq_recv[offset - 1]

    square_row = lax.fori_loop(1, n_seq, add_square, sq_send[...])
    sq_col[...] = jnp.transpose(jnp.broadcast_to(square_row[0:1], (slots, slots)))
    own_slots = pl.ds(pl.multiple_of((c * NY + y) * tq, 32), tq)
    rate = lax.rsqrt(sq_col[own_slots, 0:1] / (n_seq * states_ref.shape[1]) + EPS)
    for copy in z_copies:
        copy.wait_recv()
    total_q = zsend_q[z]
    total_kv = part[c, y, z, :, hg:]
    for dz in range(1, NZ):
        total_q += zrecv_q[dz - 1]
        total_kv += zrecv_kv[dz - 1].astype(F32)
    normed_q, normed_kv = total_q * rate, total_kv * rate
    text_rows = pl.ds(pl.multiple_of(image_keys + (c * NY + y) * tq, 32), tq)
    for h in range(n_heads):
        cols = slice(h * head, (h + 1) * head)
        x = normed_q[:, cols]
        qt[:, cols] = (x * lax.rsqrt(jnp.mean(x * x, axis=1, keepdims=True) + EPS) * qgain_ref[...]).astype(BF16)
        x = normed_kv[:, cols]
        kv[0, text_rows, cols] = (
            x * lax.rsqrt(jnp.mean(x * x, axis=1, keepdims=True) + EPS) * kgain_ref[...]
        ).astype(BF16)
    kv[1, text_rows, :] = normed_kv[:, hg:].astype(BF16)
    text_block = kv.at[:, text_rows, :]
    txkv = []
    for i, target in enumerate((s_y, s_c, s_d)):
        copy = to_seq(text_block, text_block, txkv_s.at[i], txkv_r.at[i], target)
        copy.start()
        txkv.append(copy)

    for i, q_from in ((1, q_y), (3, q_d)):
        g1[i - 1].wait_recv()
        for copy in g_ahead(i, q_from):
            copy.start()
    for dz in (0, 1, 3, 2):
        relay(dz).wait_recv()
    for copy in txkv:
        copy.wait_recv()

    length = length_ref[...].astype(F32)
    bias = jnp.where(src_row[0:1] < length, 0.0, NEG_BIG)

    def attend(query, h, near):
        cols = slice(h * head, (h + 1) * head)
        near_max, near_total, near_values = near
        image_scores = lax.dot_general(query, kv[0, far_rows, cols], NT, preferred_element_type=F32)
        text_scores = lax.dot_general(query, kv[0, image_keys:, cols], NT, preferred_element_type=F32) + bias
        top = jnp.maximum(
            jnp.max(image_scores, axis=1, keepdims=True), jnp.max(text_scores, axis=1, keepdims=True)
        )
        top = jnp.maximum(top, near_max)
        image_probs = jnp.exp2((image_scores - top) * factor)
        text_probs = jnp.exp2((text_scores - top) * factor)
        scale = jnp.exp2((near_max - top) * factor)
        denom = jnp.sum(image_probs, axis=1, keepdims=True) + jnp.sum(text_probs, axis=1, keepdims=True)
        summed = jnp.dot(image_probs.astype(BF16), kv[1, far_rows, cols], preferred_element_type=F32)
        summed += jnp.dot(text_probs.astype(BF16), kv[1, image_keys:, cols], preferred_element_type=F32)
        return (summed + scale * near_values) / (denom + scale * near_total)

    def a_block(q_from, z_of):
        return a_all.at[kv_rows(q_from, z_of), :]

    def a_return(i):
        z_to = (z + i + 1) % NZ
        return to_seq(a_block(q, z_to), a_rows.at[z], aret_s.at[i], aret_r.at[i], at_z(z_to))

    def a_plane(i):
        block = a_block(q, (z + i + 1) % NZ)
        return (
            to_seq(block, block, apl_s.at[0, i], apl_r.at[0, i], s_y),
            to_seq(block, block, apl_s.at[1, i], apl_r.at[1, i], s_c),
        )

    def a_relay(i):
        block = a_block(q_y, (z + i + 1) % NZ)
        return to_seq(block, block, apl_s.at[2, i], apl_r.at[2, i], s_c)

    def g_source(i):
        y_from = (y + i % 2) % NY
        c_from = (c + i // 2) % NC
        return y_from * NC + c_from

    @pl.loop(0, NZ)
    def _(i):
        z_to = (z + i + 1) % NZ
        for h in range(n_heads):
            cols = slice(h * head, (h + 1) * head)
            near = near_top[i, h][:, :1], near_sum[i, h][:, :1], near_acc[i, :, cols]
            result = attend(qi[z_to, :, cols], h, near)
            a_all[kv_rows(q, z_to), cols] = result.astype(BF16)

        for copy in a_plane(i):
            copy.start()

        @pl.when(i < NZ - 1)
        def _():
            a_return(i).start()

        k = (i % 2) * 2 + i // 2
        source = g_source(k)
        g_ahead(k, source)[0].wait_recv()
        g_relay(k, source).start()

        @pl.when(i > 0)
        def _():
            a_plane(i - 1)[0].wait_recv()
            a_relay(i - 1).start()

    a_rows[z] = a_all[kv_rows(q, z), :]

    slot_valid = src_col[own_slots, 0:1] < length
    for h in range(n_heads):
        cols = slice(h * head, (h + 1) * head)
        result = jnp.where(slot_valid, attend(qt[:, cols], h, attend_near(qt[:, cols], h)), 0.0)
        for zz in range(NZ):
            tsend[zz, :, cols] = result[zz * ts : (zz + 1) * ts, :]

    def t_return(dz):
        z_to = (z + dz) % NZ
        return to_seq(tsend.at[z_to], trecv.at[z], tret_s.at[dz - 1], tret_r.at[dz - 1], at_z(z_to))

    for dz in range(1, NZ):
        t_return(dz).start()
    trecv[z] = tsend[z]

    a_plane(NZ - 1)[0].wait_recv()
    a_relay(NZ - 1).start()

    for i in range(NZ - 1):
        a_return(i).wait_recv()
    image_attn = jnp.concatenate([a_rows[zz] for zz in range(NZ)], axis=1)
    per = d_model // n_seq
    for t in range(n_seq // 2):
        cols = slice(t * 2 * per, (t + 1) * 2 * per)
        projected = lax.dot_general(image_attn, wo[cols, :], NT, preferred_element_type=F32)
        image_buf[:, cols] = (gate_ref[:, cols] * projected).astype(BF16)
        term = jnp.sum(projected * dout[:, cols].astype(F32), axis=0, keepdims=True)
        gsend[2 * t, :, :per] = jnp.broadcast_to(term[:, :per], (8, per))
        gsend[2 * t + 1, :, :per] = jnp.broadcast_to(term[:, per:], (8, per))

    store_image = pltpu.make_async_copy(image_buf, image_out_ref, store_sem.at[1])
    store_image.start()

    def gate_copy(offset):
        target = (me + offset) % n_seq
        return to_seq(gsend.at[target], grecv.at[offset - 1], gg_s.at[offset - 1], gg_r.at[offset - 1], target)

    @pl.loop(1, n_seq)
    def _(offset):
        gate_copy(offset).start()

    @pl.loop(0, NZ)
    def _(i):
        source = g_source(i)
        g_ahead(i, source)[1].wait_recv()
        g_relay(i, source).wait_recv()
        a_plane(i)[1].wait_recv()
        a_relay(i).wait_recv()

    def grad_block(p):
        return jnp.dot(gt_all[p], a_all[...], preferred_element_type=F32)

    def dp_copy(jd, jz):
        p, z_to = (dp + jd) % n_dp, (z + jz) % NZ
        return pltpu.make_async_remote_copy(
            src_ref=psend.at[p, z_to],
            dst_ref=precv.at[jd, jz],
            send_sem=dp_s.at[jd, jz],
            recv_sem=dp_r.at[jd, jz],
            device_id={"dp": p, "seq": at_z(z_to)},
            device_id_type=pl.DeviceIdType.MESH,
        )

    @pl.loop(1, n_dp)
    def _(jd):
        p = (dp + jd) % n_dp
        block = grad_block(p)
        for zz in range(NZ):
            psend[p, zz] = block[zz * piece : (zz + 1) * piece].astype(BF16)
        for jz in range(NZ):
            dp_copy(jd, jz).start()

    block = grad_block(dp)
    for zz in range(NZ):
        own_grad[zz] = block[zz * piece : (zz + 1) * piece]
        psend[dp, zz] = block[zz * piece : (zz + 1) * piece].astype(BF16)
    for jz in range(1, NZ):
        dp_copy(0, jz).start()

    for dz in range(1, NZ):
        t_return(dz).wait_recv()
    for zz in range(NZ):
        text_attn_ref[:, zz * hg : (zz + 1) * hg] = trecv[zz].astype(BF16)

    def add_gate(offset, total):
        gate_copy(offset).wait_recv()
        return total + grecv[offset - 1]

    gate_total = lax.fori_loop(1, n_seq, add_gate, gsend[me])
    grad_gate_ref[...] = gate_total[0:1, :per]

    for jz in range(NZ):
        if jz:
            dp_copy(0, jz).wait_recv()
            first = precv[0, jz].astype(F32)
        else:
            first = own_grad[z]

        def add_grad(jd, total):
            dp_copy(jd, jz).wait_recv()
            return total + precv[jd, jz].astype(F32)

        fin[(z - jz + NZ) % NZ] = lax.fori_loop(1, n_dp, add_grad, first)
    for zz in range(NZ):
        grad_wo_ref[:, zz * hg : (zz + 1) * hg] = fin[zz]

    store_d_attn.wait()
    store_image.wait()
    for dz in range(1, NZ):
        for copy in kvq[dz]:
            copy.wait_send()
        t_return(dz).wait_send()
        a_return(dz - 1).wait_send()
        dp_copy(0, dz).wait_send()
    for copy in (*g1, *txkv, *y_copies, *z_copies, core_copy):
        copy.wait_send()

    @pl.loop(0, NZ)
    def _(i):
        source = g_source(i)
        for copy in (*forward(i), relay(i), *g_ahead(i, source), g_relay(i, source), *a_plane(i), a_relay(i)):
            copy.wait_send()

    @pl.loop(1, n_seq)
    def _(offset):
        square_copy(offset).wait_send()
        gate_copy(offset).wait_send()

    @pl.loop(1, n_dp)
    def _(jd):
        for jz in range(NZ):
            dp_copy(jd, jz).wait_send()


def copy_out(*refs):
    sources, results, sem = refs[:5], refs[5:10], refs[10]
    copies = [
        pltpu.make_async_copy(src, dst, sem.at[i]) for i, (src, dst) in enumerate(zip(sources, results))
    ]
    for copy in copies:
        copy.start()
    for copy in copies:
        copy.wait()


def on_device(
    n_dp,
    caption_states,
    caption_gain,
    text_proj,
    caption_len,
    slot_source,
    query_gain,
    key_gain,
    image_q,
    image_k,
    image_v,
    out_weight,
    gate,
    d_out,
):
    slots = slot_source.shape[1]
    rows, inner = image_q.shape[1:]
    d_model = d_out.shape[2]
    n_seq = NY * NZ * NC
    hg = inner // NZ
    tq = slots // NQ
    ts = tq // NZ
    blk = d_model // n_dp // NQ
    piece = blk // NZ
    per = d_model // n_seq
    vmem = pl.BlockSpec(memory_space=pltpu.VMEM)
    hbm = pl.BlockSpec(memory_space=pl.ANY)
    dma = pltpu.SemaphoreType.DMA
    sems = [
        (3,), (4,), (3, 3), (3, 3), (3, NZ), (3, NZ), (1,), (1,), (2,), (2,), (2, 3), (2, 3), (n_seq - 1,),
        (n_seq - 1,), (3,), (3,), (3,), (3,), (3, NZ), (3, NZ), (3,), (3,), (3,), (3,), (3, NZ), (3, NZ),
        (n_dp, NZ), (n_dp, NZ), (n_seq - 1,), (n_seq - 1,),
    ]
    out_shape = (
        jax.ShapeDtypeStruct((rows, d_model), BF16),
        jax.ShapeDtypeStruct((ts, inner), BF16),
        jax.ShapeDtypeStruct((rows, inner), BF16),
        jax.ShapeDtypeStruct((piece, inner), F32),
        jax.ShapeDtypeStruct((1, per), F32),
    )
    outs = pl.pallas_call(
        functools.partial(joint_kernel, n_dp),
        out_shape=out_shape,
        in_specs=[vmem, vmem, hbm, vmem, vmem, vmem, vmem, hbm, hbm, hbm, hbm, vmem, hbm],
        out_specs=(hbm, vmem, hbm, vmem, vmem),
        scratch_shapes=[
            pltpu.VMEM(text_proj.shape, BF16),
            pltpu.VMEM(out_weight.shape, BF16),
            pltpu.VMEM((rows, d_model), BF16),
            pltpu.VMEM((NC, NY, NZ, tq, 3 * hg), F32),
            pltpu.VMEM((NY, NZ, tq, 3 * hg), F32),
            *[pltpu.VMEM((n, tq, width), dtype) for n in (NZ, NZ, NZ, 3) for width, dtype in ((hg, F32), (2 * hg, BF16))],
            pltpu.VMEM((8, slots), F32),
            pltpu.VMEM((n_seq - 1, 8, slots), F32),
            pltpu.VMEM((slots, slots), F32),
            pltpu.VMEM((slots, slots), F32),
            pltpu.VMEM((NZ, rows, hg), BF16),
            pltpu.VMEM((tq, hg), BF16),
            pltpu.VMEM((NZ, hg // 128, rows, 128), F32),
            pltpu.VMEM((NZ, hg // 128, rows, 128), F32),
            pltpu.VMEM((NZ, rows, hg), F32),
            pltpu.VMEM((2, n_seq * rows + slots, hg), BF16),
            pltpu.VMEM((rows, d_model), BF16),
            pltpu.VMEM((d_model, rows), F32),
            pltpu.VMEM((NQ, n_dp, blk, rows), BF16),
            pltpu.VMEM((n_dp, blk, n_seq * rows), BF16),
            pltpu.VMEM((n_seq * rows, hg), BF16),
            pltpu.VMEM((NZ, rows, hg), BF16),
            pltpu.VMEM((NZ, ts, hg), F32),
            pltpu.VMEM((NZ, ts, hg), F32),
            pltpu.VMEM((n_dp, NZ, piece, hg), BF16),
            pltpu.VMEM((n_dp, NZ, piece, hg), BF16),
            pltpu.VMEM((NZ, piece, hg), F32),
            pltpu.VMEM((NZ, piece, hg), F32),
            pltpu.VMEM((n_seq, 8, 256), F32),
            pltpu.VMEM((n_seq - 1, 8, 256), F32),
            pltpu.VMEM((rows, d_model), BF16),
            pltpu.VMEM((rows, inner), BF16),
            dma((2,)),
            *[dma(shape) for shape in sems],
        ],
        compiler_params=pltpu.CompilerParams(
            collective_id=0, has_side_effects=True, vmem_limit_bytes=58 * 1024 * 1024
        ),
        name="joint",
    )(
        caption_states[0],
        caption_gain[None],
        text_proj,
        slot_source,
        caption_len[None],
        query_gain[None],
        key_gain[None],
        image_q[0],
        image_k[0],
        image_v[0],
        out_weight,
        gate,
        d_out[0],
    )
    image_out, text_attn, d_attn, grad_wo, grad_gate = pl.pallas_call(
        copy_out,
        out_shape=out_shape,
        in_specs=[vmem] * 5,
        out_specs=(hbm,) * 5,
        scratch_shapes=[dma((5,))],
        name="copy_out",
    )(*outs)
    return (image_out[None], text_attn[None], d_attn[None], grad_wo, grad_gate)


def solution(mesh):
    in_specs = (
        P("dp", None, "seq"),
        P("seq"),
        P("seq", None),
        P("dp"),
        P("dp", None),
        P(),
        P(),
        P("dp", "seq", None),
        P("dp", "seq", None),
        P("dp", "seq", None),
        P(),
        P("dp", None),
        P("dp", "seq", None),
    )
    out_specs = (
        P("dp", "seq", None),
        P("dp", "seq", None),
        P("dp", "seq", None),
        P(("dp", "seq"), None),
        P("dp", "seq"),
    )
    return jax.shard_map(
        functools.partial(on_device, mesh.shape["dp"]),
        mesh=mesh,
        in_specs=in_specs,
        out_specs=out_specs,
        check_vma=False,
    )
```
